32 devices in a mesh: dp: 2 (over x), fsdp: 16 (over z, y, core).
Axes of the slice: x: 2, y: 2, z: 4, core: 2. Of those that a mesh axis runs over, the one named last changes fastest.
Arguments:
- tokens: bfloat16 [32768, 1024], P(('dp', 'fsdp')), may hold values from -6 to 6
- w_query: bfloat16 [1024, 1024], P(('dp', 'fsdp')), may hold values from -0.1875 to 0.1875
- w_key: bfloat16 [1024, 1024], P(('dp', 'fsdp')), may hold values from -0.1875 to 0.1875
- w_value: bfloat16 [1024, 1024], P(('dp', 'fsdp')), may hold values from -0.1875 to 0.1875
- w_gate: bfloat16 [1024, 1024], P(('dp', 'fsdp')), may hold values from -0.1875 to 0.1875
- w_out: bfloat16 [1024, 1024], P(('dp', 'fsdp')), may hold values from -0.375 to 0.375
- w_one: bfloat16 [1024, 2816], P(('dp', 'fsdp')), may hold values from -0.1875 to 0.1875
- w_two: bfloat16 [1024, 2816], P(('dp', 'fsdp')), may hold values from -0.1875 to 0.1875
- w_three: bfloat16 [2816, 1024], P(('dp', 'fsdp')), may hold values from -0.109375 to 0.109375
- cotangent: bfloat16 [32768, 1024], P(('dp', 'fsdp')), may hold values from -6 to 6
Outputs:
- output: bfloat16 [32768, 1024], P(('dp', 'fsdp'))
- grad_tokens: bfloat16 [32768, 1024], P(('dp', 'fsdp'))
- grad_query: float32 [1024, 1024], P(('dp', 'fsdp'))
- grad_key: float32 [1024, 1024], P(('dp', 'fsdp'))
- grad_value: float32 [1024, 1024], P(('dp', 'fsdp'))
- grad_gate: float32 [1024, 1024], P(('dp', 'fsdp'))
- grad_out: float32 [1024, 1024], P(('dp', 'fsdp'))
- grad_one: float32 [1024, 2816], P(('dp', 'fsdp'))
- grad_two: float32 [1024, 2816], P(('dp', 'fsdp'))
- grad_three: float32 [2816, 1024], P(('dp', 'fsdp'))
The draws below stay inside these ranges and needn't reach their ends.
All inputs are finite; a program needn't handle non-finite values.
Results may differ from the reference program's by a relative error of at most 0.014.
Values may be sent and summed in bfloat16 or wider, within the bound.
A program may use at most 256 MiB of HBM per device.

```python
import jax
import jax.numpy as jnp
from jax import lax

D = 1024
HEADS = 16
HEAD = 64
FF = 2816
BLOCK = 128
SEQ = 1024
TOKENS = 32768


def spiked(values, own_key, source, target, parts, factor):
    owner, partner = [(jnp.arange(values.shape[dim]) // (values.shape[dim] // parts)).reshape([-1 if axis == dim else 1 for axis in range(values.ndim)]) for dim in (source, target)]
    chosen = jax.random.permutation(own_key, parts)[partner]
    strong = (owner == chosen) | (owner == (partner + parts // 2) % parts)
    return jnp.where(strong, factor * values, values)


def levels(key, shape, shards, least, largest):
    def one(position, shards_of):
        draws = jax.random.uniform(jax.random.fold_in(jax.random.fold_in(key, 6), position), (shards_of,), jnp.float32, least / len(shards), largest / len(shards))
        return jnp.repeat(jnp.exp(draws), shape[position] // shards_of).reshape((-1,) + (1,) * (len(shape) - position - 1))

    level = one(*shards[0])
    for cut in shards[1:]:
        level = level * one(*cut)
    return level


def gaussian(key, dims, spread, most, cuts=(), held_as=jnp.bfloat16):
    values = jax.random.normal(key, dims, jnp.float32) * spread
    if len(cuts) > 0:
        values = levels(key, dims, cuts, -0.22, 0.18) * values
    return jnp.clip(values, min=-most, max=most).astype(held_as)


def bell_draw_with(own_key, shape, spread, reach, cuts, heavy, held_as=jnp.bfloat16):
    entries = spread * jax.random.normal(own_key, shape, jnp.float32)
    if cuts:
        entries = entries * levels(own_key, shape, cuts, -0.22, 0.18)
    return jnp.clip(spiked(entries, jax.random.fold_in(own_key, 3), *heavy), -reach, reach).astype(held_as)


def setup_inputs(seed: int = 0) -> dict:
    arg_keys = jax.random.split(jax.random.key(seed), 11)
    return {
        "tokens": gaussian(arg_keys[0], (TOKENS, D), 1.0, 6.0, ((0, 32),)),
        "w_query": gaussian(arg_keys[1], (D, D), D ** -0.5, 0.1875, ((0, 32),)),
        "w_key": gaussian(arg_keys[2], (D, D), D ** -0.5, 0.1875, ((0, 32),)),
        "w_value": gaussian(arg_keys[3], (D, D), D ** -0.5, 0.1875, ((0, 32),)),
        "w_gate": gaussian(arg_keys[4], (D, D), D ** -0.5, 0.1875, ((0, 32),)),
        "w_out": gaussian(arg_keys[5], (D, D), (D // 4) ** -0.5, 0.375, ((0, 32),)),
        "w_one": gaussian(arg_keys[6], (D, FF), D ** -0.5, 0.1875, ((0, 32),)),
        "w_two": gaussian(arg_keys[7], (D, FF), D ** -0.5, 0.1875, ((0, 32),)),
        "w_three": gaussian(arg_keys[8], (FF, D), FF ** -0.5, 0.109375, ((0, 32),)),
        "cotangent": bell_draw_with(arg_keys[9], (TOKENS, D), 1.0, 6.0, ((0, 32),), (0, 1, 32, 2.75)),
    }


EPS = 1e-06
HIGH = lax.Precision.HIGHEST

@jax.custom_vjp
def low(v):
    return lax.optimization_barrier(v.astype(jnp.bfloat16)).astype(jnp.float32)

@jax.custom_vjp
def low_back(v):
    return v

def low_keep(v):
    return (low(v), None)

def low_pass(kept, grad):
    return (grad,)

def back_keep(v):
    return (v, None)

def back_low(kept, grad):
    return (low(grad),)
low.defvjp(low_keep, low_pass)
low_back.defvjp(back_keep, back_low)

def matmul(left, right):
    return jnp.dot(left, right, precision=HIGH, preferred_element_type=jnp.float32)

def rms_scaled(value):
    return value * lax.rsqrt(lax.optimization_barrier(jnp.mean(value * value, axis=-1, keepdims=True)) + EPS)

def logistic(value):
    return 1.0 / (1.0 + jnp.exp(-value))

def swish(value):
    return value * logistic(value)

def split_heads(value):
    return value.reshape(SEQ // BLOCK, BLOCK, HEADS, HEAD)

def attend(query, keys, values):
    q_blocks = split_heads(query)
    k_blocks = split_heads(keys)
    v_blocks = split_heads(values)
    rows_idx = lax.broadcasted_iota(jnp.int32, (BLOCK, BLOCK), 0)
    cols_idx = lax.broadcasted_iota(jnp.int32, (BLOCK, BLOCK), 1)
    raw_scores = jnp.einsum('nchd,nehd->nhce', q_blocks, k_blocks, precision=HIGH)
    scores = jnp.where(rows_idx >= cols_idx, raw_scores, jnp.zeros((), raw_scores.dtype))
    scores = low_back(low(scores))
    inner = jnp.einsum('nhce,nehd->nchd', scores, v_blocks, precision=HIGH)
    block_kv = low_back(jnp.einsum('nchd,nche->nhde', k_blocks, v_blocks, precision=HIGH))
    state = jnp.cumsum(block_kv, axis=0) - block_kv
    outer = jnp.einsum('nchd,nhde->nche', q_blocks, low(state), precision=HIGH)
    return low_back(inner + outer).reshape(SEQ, D)

def layer(x, wq, wk, wv, wu, wo, w1, w2, w3):
    normed = low(rms_scaled(x))
    query = low(swish(low_back(matmul(normed, wq))))
    keys = low(swish(low_back(matmul(normed, wk))))
    values = low(low_back(matmul(normed, wv)))
    pre_gate = low_back(matmul(normed, wu))
    attn = attend(query, keys, values)
    gated = low(rms_scaled(attn) * logistic(pre_gate))
    mid = x + low_back(matmul(gated, wo))
    normed_two = low(rms_scaled(mid))
    product = low(low_back(matmul(normed_two, w1)) * low_back(matmul(normed_two, w2)))
    return mid + low_back(matmul(product, w3))

def reference(tokens, w_query, w_key, w_value, w_gate, w_out, w_one, w_two, w_three, cotangent):
    weights = (w_query.astype(jnp.float32), w_key.astype(jnp.float32), w_value.astype(jnp.float32), w_gate.astype(jnp.float32), w_out.astype(jnp.float32), w_one.astype(jnp.float32), w_two.astype(jnp.float32), w_three.astype(jnp.float32))
    inputs = tokens.astype(jnp.float32).reshape(TOKENS // SEQ, SEQ, D)
    cotans = cotangent.astype(jnp.float32).reshape(TOKENS // SEQ, SEQ, D)

    def one_sequence(totals, item):
        x_seq, cot_seq = item
        result, pullback = jax.vjp(layer, x_seq.astype(jnp.float32), *weights)
        grads = pullback(cot_seq.astype(jnp.float32))
        summed = tuple((acc + new.astype(jnp.float32) for acc, new in zip(totals, grads[1:])))
        return (summed, (result.astype(jnp.bfloat16), grads[0].astype(jnp.bfloat16)))
    zeros = tuple((jnp.zeros(weight.shape, jnp.float32) for weight in weights))
    totals, (results, input_grads) = lax.scan(one_sequence, zeros, (inputs, cotans))
    return (results.reshape(TOKENS, D), input_grads.reshape(TOKENS, D), totals[0], totals[1], totals[2], totals[3], totals[4], totals[5], totals[6], totals[7])
```

```python
import jax
import jax.numpy as jnp
from jax import lax
from jax.sharding import PartitionSpec as P

HEADS = 16
HEAD = 64
BLOCK = 128
SEQ = 1024


EPS = 1e-06


def row_scale(value):
    return lax.rsqrt(jnp.mean(value * value, axis=-1, keepdims=True) + EPS)


def scale_back(value, scale, grad):
    return scale * grad - value * scale * scale * scale * jnp.mean(
        grad * value, axis=-1, keepdims=True
    )


def logistic(value):
    return 1.0 / (1.0 + jnp.exp(-value))


def swish_slope(value):
    sig = logistic(value)
    return sig * (1.0 + value * (1.0 - sig))


def matmul(left, right):
    return jnp.dot(left, right, preferred_element_type=jnp.float32)


def matmul_tr(left, right):
    return lax.dot_general(
        left, right, (((1,), (1,)), ((), ())), preferred_element_type=jnp.float32
    )


def weight_grad(left, right):
    return lax.dot_general(
        left, right, (((0,), (0,)), ((), ())), preferred_element_type=jnp.float32
    )


def to_blocks(value):
    return value.reshape(-1, SEQ // BLOCK, BLOCK, HEADS, HEAD)


def local(tokens, w_query, w_key, w_value, w_gate, w_out, w_one, w_two, w_three, cotangent):
    axes = ("dp", "fsdp")
    rows, width = w_query.shape
    hidden = w_one.shape[1]
    attn_all = lax.all_gather(
        jnp.concatenate((w_query, w_key, w_value, w_gate, w_out), axis=1), axes, axis=0, tiled=True
    )
    ffn_all = lax.all_gather(
        jnp.concatenate((w_one, w_two, w_three.reshape(rows, hidden)), axis=1),
        axes,
        axis=0,
        tiled=True,
    )
    wq, wk, wv, wu, wo = (attn_all[:, i * width : (i + 1) * width] for i in range(5))
    w1 = ffn_all[:, :hidden]
    w2 = ffn_all[:, hidden : 2 * hidden]
    w3 = ffn_all[:, 2 * hidden :].reshape(hidden, width)
    x = tokens.astype(jnp.float32)
    scale_one = row_scale(x)
    normed = (x * scale_one).astype(jnp.bfloat16)
    pre_q = matmul(normed, wq)
    pre_k = matmul(normed, wk)
    pre_v = matmul(normed, wv)
    pre_u = matmul(normed, wu)
    q_blocks = to_blocks((pre_q * logistic(pre_q)).astype(jnp.bfloat16))
    k_blocks = to_blocks((pre_k * logistic(pre_k)).astype(jnp.bfloat16))
    v_blocks = to_blocks(pre_v.astype(jnp.bfloat16))
    causal = jnp.tril(jnp.ones((BLOCK, BLOCK), jnp.float32))
    scores = (
        jnp.einsum("bnchd,bnehd->bnhce", q_blocks, k_blocks, preferred_element_type=jnp.float32)
        * causal
    ).astype(jnp.bfloat16)
    inner = jnp.einsum("bnhce,bnehd->bnchd", scores, v_blocks, preferred_element_type=jnp.float32)
    block_kv = jnp.einsum(
        "bnchd,bnche->bnhde", k_blocks, v_blocks, preferred_element_type=jnp.float32
    )
    state = (jnp.cumsum(block_kv, axis=1) - block_kv).astype(jnp.bfloat16)
    outer = jnp.einsum("bnchd,bnhde->bnche", q_blocks, state, preferred_element_type=jnp.float32)
    attn = (inner + outer).reshape(x.shape)
    scale_two = row_scale(attn)
    attn_normed = attn * scale_two
    sig = logistic(pre_u)
    gated = (attn_normed * sig).astype(jnp.bfloat16)
    mid = x + matmul(gated, wo)
    scale_three = row_scale(mid)
    normed_two = (mid * scale_three).astype(jnp.bfloat16)
    first = matmul(normed_two, w1)
    second = matmul(normed_two, w2)
    product = (first * second).astype(jnp.bfloat16)
    output = (mid + matmul(product, w3)).astype(jnp.bfloat16)
    grad_three = weight_grad(product, cotangent)
    dprod = matmul_tr(cotangent, w3)
    d_first = (dprod * second).astype(jnp.bfloat16)
    d_second = (dprod * first).astype(jnp.bfloat16)
    grad_one = weight_grad(normed_two, d_first)
    grad_two = weight_grad(normed_two, d_second)
    d_normed_two = matmul_tr(d_first, w1) + matmul_tr(d_second, w2)
    d_mid = cotangent.astype(jnp.float32) + scale_back(mid, scale_three, d_normed_two)
    d_branch = d_mid.astype(jnp.bfloat16)
    grad_out = weight_grad(gated, d_branch)
    d_gated = matmul_tr(d_branch, wo)
    d_pre_u = (d_gated * attn_normed * sig * (1.0 - sig)).astype(jnp.bfloat16)
    d_attn = scale_back(attn, scale_two, d_gated * sig).astype(jnp.bfloat16)
    d_blocks = to_blocks(d_attn)
    d_scores = (
        jnp.einsum("bnchd,bnehd->bnhce", d_blocks, v_blocks, preferred_element_type=jnp.float32)
        * causal
    ).astype(jnp.bfloat16)
    d_state = jnp.einsum(
        "bnchd,bnche->bnhde", q_blocks, d_blocks, preferred_element_type=jnp.float32
    )
    d_kv = (lax.cumsum(d_state, axis=1, reverse=True) - d_state).astype(jnp.bfloat16)
    dq_full = jnp.einsum(
        "bnhce,bnehd->bnchd", d_scores, k_blocks, preferred_element_type=jnp.float32
    ) + jnp.einsum("bnche,bnhde->bnchd", d_blocks, state, preferred_element_type=jnp.float32)
    dk_full = jnp.einsum(
        "bnhce,bnchd->bnehd", d_scores, q_blocks, preferred_element_type=jnp.float32
    ) + jnp.einsum("bnche,bnhde->bnchd", v_blocks, d_kv, preferred_element_type=jnp.float32)
    dv_full = jnp.einsum(
        "bnhce,bnchd->bnehd", scores, d_blocks, preferred_element_type=jnp.float32
    ) + jnp.einsum("bnchd,bnhde->bnche", k_blocks, d_kv, preferred_element_type=jnp.float32)
    d_query = (dq_full.reshape(x.shape) * swish_slope(pre_q)).astype(jnp.bfloat16)
    d_key = (dk_full.reshape(x.shape) * swish_slope(pre_k)).astype(jnp.bfloat16)
    d_value = dv_full.reshape(x.shape).astype(jnp.bfloat16)
    grad_query = weight_grad(normed, d_query)
    grad_key = weight_grad(normed, d_key)
    grad_value = weight_grad(normed, d_value)
    grad_gate = weight_grad(normed, d_pre_u)
    d_normed = (
        matmul_tr(d_query, wq)
        + matmul_tr(d_key, wk)
        + matmul_tr(d_value, wv)
        + matmul_tr(d_pre_u, wu)
    )
    grad_tokens = (d_mid + scale_back(x, scale_one, d_normed)).astype(jnp.bfloat16)
    half = jnp.bfloat16
    ffn_grads = jnp.concatenate(
        (
            grad_one.astype(half),
            grad_two.astype(half),
            grad_three.astype(half).reshape(width, hidden),
        ),
        axis=1,
    )
    attn_grads = jnp.concatenate(
        [g.astype(half) for g in (grad_query, grad_key, grad_value, grad_gate, grad_out)], axis=1
    )
    ffn_sum = lax.psum_scatter(ffn_grads, axes, scatter_dimension=0, tiled=True)
    attn_sum = lax.psum_scatter(attn_grads, axes, scatter_dimension=0, tiled=True)
    ffn_sum = ffn_sum.astype(jnp.float32)
    attn_sum = attn_sum.astype(jnp.float32)
    shares = tuple(attn_sum[:, i * width : (i + 1) * width] for i in range(5)) + (
        ffn_sum[:, :hidden],
        ffn_sum[:, hidden : 2 * hidden],
        ffn_sum[:, 2 * hidden :].reshape(w_three.shape),
    )
    return (
        output,
        grad_tokens,
        shares[0],
        shares[1],
        shares[2],
        shares[3],
        shares[4],
        shares[5],
        shares[6],
        shares[7],
    )


def solution(mesh):
    in_specs = (
        P(("dp", "fsdp"), None),
        P(("dp", "fsdp"), None),
        P(("dp", "fsdp"), None),
        P(("dp", "fsdp"), None),
        P(("dp", "fsdp"), None),
        P(("dp", "fsdp"), None),
        P(("dp", "fsdp"), None),
        P(("dp", "fsdp"), None),
        P(("dp", "fsdp"), None),
        P(("dp", "fsdp"), None),
    )
    out_specs = (
        P(("dp", "fsdp"), None),
        P(("dp", "fsdp"), None),
        P(("dp", "fsdp"), None),
        P(("dp", "fsdp"), None),
        P(("dp", "fsdp"), None),
        P(("dp", "fsdp"), None),
        P(("dp", "fsdp"), None),
        P(("dp", "fsdp"), None),
        P(("dp", "fsdp"), None),
        P(("dp", "fsdp"), None),
    )
    return jax.shard_map(local, mesh=mesh, in_specs=in_specs, out_specs=out_specs, check_vma=False)
```

```python
import functools

import jax
import jax.numpy as jnp
from jax import lax
from jax.experimental import pallas as pl
from jax.experimental.pallas import tpu as pltpu
from jax.sharding import PartitionSpec as P

HEADS = 16
HEAD = 64
BLOCK = 128
SEQ = 1024
SPAN = 256
EPS = 1e-06
MESH = pl.DeviceIdType.MESH
F32 = jnp.float32
BF16 = jnp.bfloat16


def row_scale(value):
    return lax.rsqrt(jnp.mean(value * value, axis=-1, keepdims=True) + EPS)


def scale_back(value, scale, grad):
    return scale * grad - value * scale * scale * scale * jnp.mean(
        grad * value, axis=-1, keepdims=True
    )


def logistic(value):
    return 1.0 / (1.0 + jnp.exp(-value))


def swish_slope(value):
    sig = logistic(value)
    return sig * (1.0 + value * (1.0 - sig))


def matmul(left, right):
    return jnp.dot(left, right, preferred_element_type=jnp.float32)


def matmul_tr(left, right):
    return lax.dot_general(
        left, right, (((1,), (1,)), ((), ())), preferred_element_type=jnp.float32
    )


def weight_grad(left, right):
    return lax.dot_general(
        left, right, (((0,), (0,)), ((), ())), preferred_element_type=jnp.float32
    )


class Cube:
    def __init__(self, nd, nf):
        self.nd, self.nf = nd, nf
        self.kd, self.kf = nd.bit_length() - 1, nf.bit_length() - 1
        self.k = self.kd + self.kf
        top = [self.kf - 1, self.kf - 2]
        outer = list(range(self.kf, self.k))
        mid = list(range(self.kf - 3, 0, -1))
        self.kinds = (
            (top + outer + mid + [0], top + mid + outer + [0]),
            (outer + top + mid + [0], mid + top + outer + [0]),
        )

    def place(self):
        self.x, self.f = lax.axis_index("dp"), lax.axis_index("fsdp")
        index = self.x * self.nf + self.f
        self.bits = [(index // (1 << b)) % 2 for b in range(self.k)]

    def partner(self, b):
        step = 1 - 2 * self.bits[b]
        if b < self.kf:
            return (self.x, self.f + step * (1 << b))
        return (self.x + step * (1 << (b - self.kf)), self.f)

    def at(self, free, flip=None):
        return tuple(
            slice(None) if b in free else (1 - self.bits[b] if b == flip else self.bits[b])
            for b in range(self.k - 1, -1, -1)
        )

    def barrier(self):
        sem = pltpu.get_barrier_semaphore()
        for b in range(self.k):
            pl.semaphore_signal(sem, inc=1, device_id=self.partner(b), device_id_type=MESH)
        pl.semaphore_wait(sem, self.k)


def at_row(i, size):
    return pl.ds(pl.multiple_of(i * size, size), size)


def head_masks(shape):
    lane = lax.broadcasted_iota(jnp.int32, shape, len(shape) - 1)
    return lane < HEAD


def two_heads(value):
    low = head_masks(value.shape)
    zero = jnp.zeros_like(value)
    return jnp.concatenate([jnp.where(low, value, zero), jnp.where(low, zero, value)], axis=0)


def pick_heads(value):
    rows = value.shape[0] // 2
    upper, lower = value[:rows], value[rows:]
    return jnp.where(head_masks(upper.shape), upper, lower)


def causal_pair():
    row = lax.broadcasted_iota(jnp.int32, (SPAN, 2 * SPAN), 0)
    col = lax.broadcasted_iota(jnp.int32, (SPAN, 2 * SPAN), 1)
    return row >= jnp.where(col >= SPAN, col - SPAN, col)


def same_head(value):
    row = lax.broadcasted_iota(jnp.int32, value.shape, 0)
    col = lax.broadcasted_iota(jnp.int32, value.shape, 1)
    return jnp.where((row < HEAD) == (col < HEAD), value, jnp.zeros_like(value))


def to_blocks(value):
    return value.reshape(-1, SEQ // BLOCK, BLOCK, HEADS, HEAD)


def plain_local(tokens, w_query, w_key, w_value, w_gate, w_out, w_one, w_two, w_three, cotangent):
    axes = ("dp", "fsdp")
    rows, width = w_query.shape
    hidden = w_one.shape[1]
    attn_all = lax.all_gather(
        jnp.concatenate((w_query, w_key, w_value, w_gate, w_out), axis=1), axes, axis=0, tiled=True
    )
    ffn_all = lax.all_gather(
        jnp.concatenate((w_one, w_two, w_three.reshape(rows, hidden)), axis=1),
        axes,
        axis=0,
        tiled=True,
    )
    wq, wk, wv, wu, wo = (attn_all[:, i * width : (i + 1) * width] for i in range(5))
    w1 = ffn_all[:, :hidden]
    w2 = ffn_all[:, hidden : 2 * hidden]
    w3 = ffn_all[:, 2 * hidden :].reshape(hidden, width)
    x = tokens.astype(jnp.float32)
    scale_one = row_scale(x)
    normed = (x * scale_one).astype(jnp.bfloat16)
    pre_q = matmul(normed, wq)
    pre_k = matmul(normed, wk)
    pre_v = matmul(normed, wv)
    pre_u = matmul(normed, wu)
    q_blocks = to_blocks((pre_q * logistic(pre_q)).astype(jnp.bfloat16))
    k_blocks = to_blocks((pre_k * logistic(pre_k)).astype(jnp.bfloat16))
    v_blocks = to_blocks(pre_v.astype(jnp.bfloat16))
    causal = jnp.tril(jnp.ones((BLOCK, BLOCK), jnp.float32))
    scores = (
        jnp.einsum("bnchd,bnehd->bnhce", q_blocks, k_blocks, preferred_element_type=jnp.float32)
        * causal
    ).astype(jnp.bfloat16)
    inner = jnp.einsum("bnhce,bnehd->bnchd", scores, v_blocks, preferred_element_type=jnp.float32)
    block_kv = jnp.einsum(
        "bnchd,bnche->bnhde", k_blocks, v_blocks, preferred_element_type=jnp.float32
    )
    state = (jnp.cumsum(block_kv, axis=1) - block_kv).astype(jnp.bfloat16)
    outer = jnp.einsum("bnchd,bnhde->bnche", q_blocks, state, preferred_element_type=jnp.float32)
    attn = (inner + outer).reshape(x.shape)
    scale_two = row_scale(attn)
    attn_normed = attn * scale_two
    sig = logistic(pre_u)
    gated = (attn_normed * sig).astype(jnp.bfloat16)
    mid = x + matmul(gated, wo)
    scale_three = row_scale(mid)
    normed_two = (mid * scale_three).astype(jnp.bfloat16)
    first = matmul(normed_two, w1)
    second = matmul(normed_two, w2)
    product = (first * second).astype(jnp.bfloat16)
    output = (mid + matmul(product, w3)).astype(jnp.bfloat16)
    grad_three = weight_grad(product, cotangent)
    dprod = matmul_tr(cotangent, w3)
    d_first = (dprod * second).astype(jnp.bfloat16)
    d_second = (dprod * first).astype(jnp.bfloat16)
    grad_one = weight_grad(normed_two, d_first)
    grad_two = weight_grad(normed_two, d_second)
    d_normed_two = matmul_tr(d_first, w1) + matmul_tr(d_second, w2)
    d_mid = cotangent.astype(jnp.float32) + scale_back(mid, scale_three, d_normed_two)
    d_branch = d_mid.astype(jnp.bfloat16)
    grad_out = weight_grad(gated, d_branch)
    d_gated = matmul_tr(d_branch, wo)
    d_pre_u = (d_gated * attn_normed * sig * (1.0 - sig)).astype(jnp.bfloat16)
    d_attn = scale_back(attn, scale_two, d_gated * sig).astype(jnp.bfloat16)
    d_blocks = to_blocks(d_attn)
    d_scores = (
        jnp.einsum("bnchd,bnehd->bnhce", d_blocks, v_blocks, preferred_element_type=jnp.float32)
        * causal
    ).astype(jnp.bfloat16)
    d_state = jnp.einsum(
        "bnchd,bnche->bnhde", q_blocks, d_blocks, preferred_element_type=jnp.float32
    )
    d_kv = (lax.cumsum(d_state, axis=1, reverse=True) - d_state).astype(jnp.bfloat16)
    dq_full = jnp.einsum(
        "bnhce,bnehd->bnchd", d_scores, k_blocks, preferred_element_type=jnp.float32
    ) + jnp.einsum("bnche,bnhde->bnchd", d_blocks, state, preferred_element_type=jnp.float32)
    dk_full = jnp.einsum(
        "bnhce,bnchd->bnehd", d_scores, q_blocks, preferred_element_type=jnp.float32
    ) + jnp.einsum("bnche,bnhde->bnchd", v_blocks, d_kv, preferred_element_type=jnp.float32)
    dv_full = jnp.einsum(
        "bnhce,bnchd->bnehd", scores, d_blocks, preferred_element_type=jnp.float32
    ) + jnp.einsum("bnchd,bnhde->bnche", k_blocks, d_kv, preferred_element_type=jnp.float32)
    d_query = (dq_full.reshape(x.shape) * swish_slope(pre_q)).astype(jnp.bfloat16)
    d_key = (dk_full.reshape(x.shape) * swish_slope(pre_k)).astype(jnp.bfloat16)
    d_value = dv_full.reshape(x.shape).astype(jnp.bfloat16)
    grad_query = weight_grad(normed, d_query)
    grad_key = weight_grad(normed, d_key)
    grad_value = weight_grad(normed, d_value)
    grad_gate = weight_grad(normed, d_pre_u)
    d_normed = (
        matmul_tr(d_query, wq)
        + matmul_tr(d_key, wk)
        + matmul_tr(d_value, wv)
        + matmul_tr(d_pre_u, wu)
    )
    grad_tokens = (d_mid + scale_back(x, scale_one, d_normed)).astype(jnp.bfloat16)
    half = jnp.bfloat16
    ffn_grads = jnp.concatenate(
        (
            grad_one.astype(half),
            grad_two.astype(half),
            grad_three.astype(half).reshape(width, hidden),
        ),
        axis=1,
    )
    attn_grads = jnp.concatenate(
        [g.astype(half) for g in (grad_query, grad_key, grad_value, grad_gate, grad_out)], axis=1
    )
    ffn_sum = lax.psum_scatter(ffn_grads, axes, scatter_dimension=0, tiled=True)
    attn_sum = lax.psum_scatter(attn_grads, axes, scatter_dimension=0, tiled=True)
    ffn_sum = ffn_sum.astype(jnp.float32)
    attn_sum = attn_sum.astype(jnp.float32)
    shares = tuple(attn_sum[:, i * width : (i + 1) * width] for i in range(5)) + (
        ffn_sum[:, :hidden],
        ffn_sum[:, hidden : 2 * hidden],
        ffn_sum[:, 2 * hidden :].reshape(w_three.shape),
    )
    return (
        output,
        grad_tokens,
        shares[0],
        shares[1],
        shares[2],
        shares[3],
        shares[4],
        shares[5],
        shares[6],
        shares[7],
    )


class Copies:
    def __init__(self, sems):
        self.sems, self.count = sems, 0

    def start(self, src, dst):
        copy = pltpu.make_async_copy(src, dst, self.sems.at[self.count])
        self.count += 1
        copy.start()
        return copy


def forward_chunks(width, hidden):
    chunks = []
    for t in range(5):
        chunks += [(t, c, width // 2) for c in range(0, width, width // 2)]
    for c in range(0, hidden, width):
        size = min(width, hidden - c)
        chunks += [(5, c, size), (6, c, size)]
    chunks += [(7, c, 256) for c in range(0, width, 256)]
    return chunks


SLOTS, SLOTS3, SPACING = 5, 3, 2
ACTS = ("nrm", "q", "sq", "k", "sk", "v", "u", "att", "y", "mid", "n2", "g1", "g2", "prod", "out")


def forward_kernel(cube, chunks, *refs):
    tok, shards = refs[0], refs[1:9]
    weights = refs[9:17]
    acts = dict(zip(ACTS, refs[17 : 17 + len(ACTS)]))
    (nb, a1, a2, a3, fu, fa, fm, stage, stage3, send, recv, own, local) = refs[17 + len(ACTS) :]
    cube.place()
    core, k, n = cube.bits[0], cube.k, len(chunks)
    width = tok.shape[1]
    mine = []
    for t in range(8):
        mine.append(pltpu.make_async_copy(shards[t], weights[t].at[cube.at(())], own.at[t]))
        mine[-1].start()
    cube.barrier()
    copies = Copies(local)


    def copy(c, s, v):
        t, c0, w = chunks[c]
        order = cube.kinds[c % 2][v]
        where = cube.at(order[:s]) + (slice(None), pl.ds(c0, w))
        src = shards[t].at[:, pl.ds(c0, w)] if s == 0 else weights[t].at[where]
        return pltpu.make_async_remote_copy(
            src_ref=src,
            dst_ref=weights[t].at[where],
            send_sem=send.at[c, s],
            recv_sem=recv.at[c, s],
            device_id=cube.partner(order[s]),
            device_id_type=MESH,
        )

    def both(c, s, act):
        first, second = cube.kinds[c % 2]
        if first[s] == second[s] and set(first[:s]) == set(second[:s]):
            act(copy(c, s, 0))
        else:

            @pl.when(core == 0)
            def _():
                act(copy(c, s, 0))

            @pl.when(core == 1)
            def _():
                act(copy(c, s, 1))


    whole = (slice(None),) * (k + 1)
    pending = {}

    def out_of(name, src):
        pending[name] = copies.start(src, acts[name])

    def settle(*names):
        for name in names:
            if name in pending:
                pending.pop(name).wait()

    def cols(ref, c, w):
        return ref[whole + (pl.ds(pl.multiple_of(c, 256), w),)].reshape(-1, w)

    def tiles(total, body):
        def step(i, carry):
            body(i // 2, i % 2)
            return carry

        lax.fori_loop(0, total // 256 * 2, step, 0)

    def rows(body, size=128):
        def step(i, carry):
            body(at_row(i, size))
            return carry

        lax.fori_loop(0, SEQ // size, step, 0)

    def norm_one():
        def body(r):
            x = tok[r, :].astype(F32)
            nb[r, :] = (x * row_scale(x)).astype(BF16)

        rows(body)
        out_of("nrm", nb)

    def project(t, c0, w, ref):
        def body(j, h):
            r = at_row(h, 512)
            to = pl.ds(pl.multiple_of(c0 + j * 256, 256), 256)
            acc = matmul(nb[r, :], cols(ref, j * 256, 256))
            if t == 3:
                fu[r, to] = acc
            elif t == 2:
                a3[r, to] = acc.astype(BF16)
            else:
                slope_to = pl.ds(pl.multiple_of(width + c0 + j * 256, 256), 256)
                sig = logistic(acc)
                dst = a1 if t == 0 else a2
                dst[r, to] = (acc * sig).astype(BF16)
                dst[r, slope_to] = (sig * (1.0 + acc * (1.0 - sig))).astype(BF16)

        tiles(w, body)
        if c0 + w == width:
            if t == 3:
                out_of("u", fu)
            elif t == 2:
                out_of("v", a3.at[:, pl.ds(0, width)])
            else:
                src = a1 if t == 0 else a2
                out_of("qk"[t], src.at[:, pl.ds(0, width)])
                out_of(("sq", "sk")[t], src.at[:, pl.ds(width, width)])

    def attend(first, last):
        mask = causal_pair()

        def pair(p, carry):
            at = pl.ds(pl.multiple_of(p * 128, 128), 128)
            state = jnp.zeros((128, 128), F32)
            for b in range(SEQ // SPAN):
                r = pl.ds(b * SPAN, SPAN)
                q, kk, v = a1[r, at], a2[r, at], a3[r, at]
                scores = jnp.where(mask, matmul_tr(q, two_heads(kk)), 0.0).astype(BF16)
                acc = matmul(scores, two_heads(v))
                if b > 0:
                    acc += matmul(q, state.astype(BF16))
                fa[r, at] = acc
                if b + 1 < SEQ // SPAN:
                    state += same_head(weight_grad(kk, v))
            return carry

        lax.fori_loop(first, last, pair, 0)
        if last == width // 128:
            out_of("att", fa)

    def gate():
        def body(r):
            attn = fa[r, :]
            a3[r, pl.ds(width, width)] = (attn * row_scale(attn) * logistic(fu[r, :])).astype(BF16)

        rows(body)
        out_of("y", a3.at[:, pl.ds(width, width)])

    def project_out(c0, w, ref):
        def body(j, h):
            r = at_row(h, 512)
            to = pl.ds(pl.multiple_of(c0 + j * 256, 256), 256)
            fm[r, to] = tok[r, to].astype(F32) + matmul(
                a3[r, pl.ds(width, width)], cols(ref, j * 256, 256)
            )

        tiles(w, body)

    def norm_two():
        settle("nrm")

        def body(r):
            mid = fm[r, :]
            nb[r, :] = (mid * row_scale(mid)).astype(BF16)

        rows(body)
        out_of("mid", fm)
        out_of("n2", nb)
        settle("q", "sq", "k", "sk", "v", "y")

    def hidden(c0, w, one, two):
        def body(j, h):
            r = at_row(h, 512)
            to = pl.ds(pl.multiple_of(c0 + j * 256, 256), 256)
            first = matmul(nb[r, :], cols(one, j * 256, 256))
            second = matmul(nb[r, :], cols(two, j * 256, 256))
            a1[r, to] = first.astype(BF16)
            a2[r, to] = second.astype(BF16)
            a3[r, to] = (first * second).astype(BF16)

        tiles(w, body)
        if c0 + w == a1.shape[1]:
            out_of("g1", a1)
            out_of("g2", a2)
            out_of("prod", a3)
            settle("n2")

    def down(c0, w, ref):
        def body(j, h):
            r = at_row(h, 512)
            to = pl.ds(pl.multiple_of(c0 + j * 256, 256), 256)
            nb[r, to] = (fm[r, to] + matmul(a3[r, :], cols(ref, j * 256, 256))).astype(BF16)

        tiles(w, body)
        if c0 + w == width:
            out_of("out", nb)

    index = {(t, c0): i for i, (t, c0, w) in enumerate(chunks)}
    items = [((), norm_one)]
    for i, (t, c0, w) in enumerate(chunks):
        last = c0 + w == width
        if t < 4:
            items.append(((i,), functools.partial(project, t, c0, w)))
            if t == 2 and last:
                items += [((), functools.partial(attend, 0, 4)), ((), functools.partial(attend, 4, 8))]
            if t == 3 and last:
                items.append(((), gate))
        elif t == 4:
            items.append(((i,), functools.partial(project_out, c0, w)))
            if last:
                items.append(((), norm_two))
        elif t == 5:
            items.append(((i, index[6, c0]), functools.partial(hidden, c0, w)))
        elif t == 7:
            items.append(((i,), functools.partial(down, c0, w)))

    free = {False: list(range(SLOTS)), True: list(range(SLOTS3))}
    arrived, staged = [], {}

    def stage_some(tick):
        while arrived and free[chunks[arrived[0]][0] == 7]:
            c = arrived.pop(0)
            t, c0, w = chunks[c]
            slot = free[t == 7].pop(0)
            dst = (stage3 if t == 7 else stage).at[(slot,) + whole + (pl.ds(0, w),)]
            cp = copies.start(weights[t].at[whole + (pl.ds(c0, w),)], dst)
            staged[c] = (tick, slot, cp)

    def run(tick, budget):
        while items and budget > 0:
            needs, act = items[0]
            if any(c not in staged or staged[c][0] >= tick for c in needs):
                return
            items.pop(0)
            given = []
            for c in needs:
                _, slot, cp = staged[c]
                cp.wait()
                given.append((stage3 if chunks[c][0] == 7 else stage).at[slot])
            act(*given)
            for c in needs:
                free[chunks[c][0] == 7].append(staged[c][1])
            budget -= 1

    settled = set()
    ticks = n + k * SPACING
    for tick in range(ticks):
        for c in range(n):
            d = tick - c
            if d < 0 or d % SPACING or d // SPACING > k:
                continue
            s = d // SPACING
            if s > 0:
                both(c, s - 1, lambda cp: cp.wait_recv())
            if s == 1 and chunks[c][0] not in settled:
                settled.add(chunks[c][0])
                mine[chunks[c][0]].wait()
            if s < k:
                both(c, s, lambda cp: cp.start())
            else:
                arrived.append(c)
        run(tick, 2)
        stage_some(tick)
    tick = ticks
    while items:
        run(tick, 1)
        stage_some(tick)
        tick += 1
    for c in range(n):
        for s in range(k):
            both(c, s, lambda cp: cp.wait_send())
    settle(*list(pending))


def forward(cube, tokens, shards):
    width, hidden = tokens.shape[1], shards[5].shape[1]
    chunks = forward_chunks(width, hidden)
    n, k = len(chunks), cube.k
    cubed = (2,) * k
    act = lambda dtype: jax.ShapeDtypeStruct(tokens.shape, dtype)
    kinds = dict.fromkeys(("u", "att", "mid"), act(F32))
    kinds.update(dict.fromkeys(("g1", "g2", "prod"), jax.ShapeDtypeStruct((SEQ, hidden), BF16)))
    outs = [jax.ShapeDtypeStruct(cubed + s.shape, s.dtype) for s in shards]
    outs += [kinds.get(name, act(BF16)) for name in ACTS]
    got = pl.pallas_call(
        functools.partial(forward_kernel, cube, chunks),
        out_shape=tuple(outs),
        in_specs=[pl.BlockSpec(memory_space=pltpu.VMEM)] * 9,
        out_specs=tuple([pl.BlockSpec(memory_space=pl.ANY)] * len(outs)),
        scratch_shapes=[
            pltpu.VMEM(tokens.shape, BF16),
            pltpu.VMEM((SEQ, hidden), BF16),
            pltpu.VMEM((SEQ, hidden), BF16),
            pltpu.VMEM((SEQ, hidden), BF16),
            pltpu.VMEM(tokens.shape, F32),
            pltpu.VMEM(tokens.shape, F32),
            pltpu.VMEM(tokens.shape, F32),
            pltpu.VMEM((SLOTS,) + cubed + (shards[0].shape[0], width), BF16),
            pltpu.VMEM((SLOTS3,) + cubed + (shards[7].shape[0], 256), BF16),
            pltpu.SemaphoreType.DMA((n, k)),
            pltpu.SemaphoreType.DMA((n, k)),
            pltpu.SemaphoreType.DMA((8,)),
            pltpu.SemaphoreType.DMA((n + len(ACTS),)),
        ],
        compiler_params=pltpu.CompilerParams(
            collective_id=0, has_side_effects=True, vmem_limit_bytes=64 * 1024 * 1024 - 65536
        ),
        name="gather_and_forward",
    )(tokens, *shards)
    return got[:8], dict(zip(ACTS, got[8:]))


def local(cube, tokens, w_query, w_key, w_value, w_gate, w_out, w_one, w_two, w_three, cotangent):
    shards = (w_query, w_key, w_value, w_gate, w_out, w_one, w_two, w_three)
    axes = ("dp", "fsdp")
    width, hidden = w_one.shape[0] * cube.nd * cube.nf, w_one.shape[1]
    gathered, acts = forward(cube, tokens, shards)
    wq, wk, wv, wu, wo, w1, w2, w3 = (w.reshape(-1, w.shape[-1]) for w in gathered)
    x = tokens.astype(F32)
    scale_one = row_scale(x)
    normed, normed_two, gated, product = acts["nrm"], acts["n2"], acts["y"], acts["prod"]
    first, second = acts["g1"].astype(F32), acts["g2"].astype(F32)
    mid, attn, output = acts["mid"], acts["att"], acts["out"]
    scale_two, scale_three = row_scale(attn), row_scale(mid)
    attn_normed, sig = attn * scale_two, logistic(acts["u"])
    q_blocks, k_blocks, v_blocks = to_blocks(acts["q"]), to_blocks(acts["k"]), to_blocks(acts["v"])
    causal = jnp.tril(jnp.ones((BLOCK, BLOCK), jnp.float32))
    scores = (
        jnp.einsum("bnchd,bnehd->bnhce", q_blocks, k_blocks, preferred_element_type=jnp.float32)
        * causal
    ).astype(jnp.bfloat16)
    block_kv = jnp.einsum(
        "bnchd,bnche->bnhde", k_blocks, v_blocks, preferred_element_type=jnp.float32
    )
    state = (jnp.cumsum(block_kv, axis=1) - block_kv).astype(jnp.bfloat16)
    grad_three = weight_grad(product, cotangent)
    dprod = matmul_tr(cotangent, w3)
    d_first = (dprod * second).astype(jnp.bfloat16)
    d_second = (dprod * first).astype(jnp.bfloat16)
    grad_one = weight_grad(normed_two, d_first)
    grad_two = weight_grad(normed_two, d_second)
    d_normed_two = matmul_tr(d_first, w1) + matmul_tr(d_second, w2)
    d_mid = cotangent.astype(jnp.float32) + scale_back(mid, scale_three, d_normed_two)
    d_branch = d_mid.astype(jnp.bfloat16)
    grad_out = weight_grad(gated, d_branch)
    d_gated = matmul_tr(d_branch, wo)
    d_pre_u = (d_gated * attn_normed * sig * (1.0 - sig)).astype(jnp.bfloat16)
    d_attn = scale_back(attn, scale_two, d_gated * sig).astype(jnp.bfloat16)
    d_blocks = to_blocks(d_attn)
    d_scores = (
        jnp.einsum("bnchd,bnehd->bnhce", d_blocks, v_blocks, preferred_element_type=jnp.float32)
        * causal
    ).astype(jnp.bfloat16)
    d_state = jnp.einsum(
        "bnchd,bnche->bnhde", q_blocks, d_blocks, preferred_element_type=jnp.float32
    )
    d_kv = (lax.cumsum(d_state, axis=1, reverse=True) - d_state).astype(jnp.bfloat16)
    dq_full = jnp.einsum(
        "bnhce,bnehd->bnchd", d_scores, k_blocks, preferred_element_type=jnp.float32
    ) + jnp.einsum("bnche,bnhde->bnchd", d_blocks, state, preferred_element_type=jnp.float32)
    dk_full = jnp.einsum(
        "bnhce,bnchd->bnehd", d_scores, q_blocks, preferred_element_type=jnp.float32
    ) + jnp.einsum("bnche,bnhde->bnchd", v_blocks, d_kv, preferred_element_type=jnp.float32)
    dv_full = jnp.einsum(
        "bnhce,bnchd->bnehd", scores, d_blocks, preferred_element_type=jnp.float32
    ) + jnp.einsum("bnchd,bnhde->bnche", k_blocks, d_kv, preferred_element_type=jnp.float32)
    d_query = (dq_full.reshape(tokens.shape) * acts["sq"]).astype(jnp.bfloat16)
    d_key = (dk_full.reshape(tokens.shape) * acts["sk"]).astype(jnp.bfloat16)
    d_value = dv_full.reshape(tokens.shape).astype(jnp.bfloat16)
    grad_query = weight_grad(normed, d_query)
    grad_key = weight_grad(normed, d_key)
    grad_value = weight_grad(normed, d_value)
    grad_gate = weight_grad(normed, d_pre_u)
    d_normed = (
        matmul_tr(d_query, wq)
        + matmul_tr(d_key, wk)
        + matmul_tr(d_value, wv)
        + matmul_tr(d_pre_u, wu)
    )
    grad_tokens = (d_mid + scale_back(x, scale_one, d_normed)).astype(jnp.bfloat16)
    half = jnp.bfloat16
    ffn_grads = jnp.concatenate(
        (
            grad_one.astype(half),
            grad_two.astype(half),
            grad_three.astype(half).reshape(width, hidden),
        ),
        axis=1,
    )
    attn_grads = jnp.concatenate(
        [g.astype(half) for g in (grad_query, grad_key, grad_value, grad_gate, grad_out)], axis=1
    )
    ffn_sum = lax.psum_scatter(ffn_grads, axes, scatter_dimension=0, tiled=True)
    attn_sum = lax.psum_scatter(attn_grads, axes, scatter_dimension=0, tiled=True)
    ffn_sum = ffn_sum.astype(jnp.float32)
    attn_sum = attn_sum.astype(jnp.float32)
    shares = tuple(attn_sum[:, i * width : (i + 1) * width] for i in range(5)) + (
        ffn_sum[:, :hidden],
        ffn_sum[:, hidden : 2 * hidden],
        ffn_sum[:, 2 * hidden :].reshape(w_three.shape),
    )
    return (
        output,
        grad_tokens,
        shares[0],
        shares[1],
        shares[2],
        shares[3],
        shares[4],
        shares[5],
        shares[6],
        shares[7],
    )


def solution(mesh):
    nd, nf = mesh.shape["dp"], mesh.shape["fsdp"]
    rows = P(("dp", "fsdp"), None)

    def step(*args):
        fits = args[1].shape[0] % 16 == 0 and args[8].shape[0] % 8 == 0 and args[0].shape[0] == SEQ
        if fits:
            return local(Cube(nd, nf), *args)
        return plain_local(*args)

    return jax.shard_map(
        step, mesh=mesh, in_specs=(rows,) * 10, out_specs=(rows,) * 10, check_vma=False
    )
```

```python
import functools

import jax
import jax.numpy as jnp
from jax import lax
from jax.experimental import pallas as pl
from jax.experimental.pallas import tpu as pltpu
from jax.sharding import PartitionSpec as P

HEADS = 16
HEAD = 64
BLOCK = 128
SEQ = 1024
SPAN = 256
EPS = 1e-06
MESH = pl.DeviceIdType.MESH
F32 = jnp.float32
BF16 = jnp.bfloat16


def row_scale(value):
    return lax.rsqrt(jnp.mean(value * value, axis=-1, keepdims=True) + EPS)


def scale_back(value, scale, grad):
    return scale * grad - value * scale * scale * scale * jnp.mean(
        grad * value, axis=-1, keepdims=True
    )


def logistic(value):
    return 1.0 / (1.0 + jnp.exp(-value))


def swish_slope(value):
    sig = logistic(value)
    return sig * (1.0 + value * (1.0 - sig))


def matmul(left, right):
    return jnp.dot(left, right, preferred_element_type=jnp.float32)


def matmul_tr(left, right):
    return lax.dot_general(
        left, right, (((1,), (1,)), ((), ())), preferred_element_type=jnp.float32
    )


def weight_grad(left, right):
    return lax.dot_general(
        left, right, (((0,), (0,)), ((), ())), preferred_element_type=jnp.float32
    )


class Cube:
    def __init__(self, nd, nf):
        self.nd, self.nf = nd, nf
        self.kd, self.kf = nd.bit_length() - 1, nf.bit_length() - 1
        self.k = self.kd + self.kf
        top = [self.kf - 1, self.kf - 2]
        outer = list(range(self.kf, self.k))
        mid = list(range(self.kf - 3, 0, -1))
        self.kinds = (
            (top + outer + mid + [0], top + mid + outer + [0]),
            (outer + top + mid + [0], mid + top + outer + [0]),
        )

    def place(self):
        self.x, self.f = lax.axis_index("dp"), lax.axis_index("fsdp")
        index = self.x * self.nf + self.f
        self.bits = [(index // (1 << b)) % 2 for b in range(self.k)]

    def partner(self, b):
        step = 1 - 2 * self.bits[b]
        if b < self.kf:
            return (self.x, self.f + step * (1 << b))
        return (self.x + step * (1 << (b - self.kf)), self.f)

    def at(self, free, flip=None):
        return tuple(
            slice(None) if b in free else (1 - self.bits[b] if b == flip else self.bits[b])
            for b in range(self.k - 1, -1, -1)
        )

    def barrier(self):
        sem = pltpu.get_barrier_semaphore()
        for b in range(self.k):
            pl.semaphore_signal(sem, inc=1, device_id=self.partner(b), device_id_type=MESH)
        pl.semaphore_wait(sem, self.k)


def at_row(i, size):
    return pl.ds(pl.multiple_of(i * size, size), size)


def head_masks(shape):
    lane = lax.broadcasted_iota(jnp.int32, shape, len(shape) - 1)
    return lane < HEAD


def two_heads(value):
    low = head_masks(value.shape)
    zero = jnp.zeros_like(value)
    return jnp.concatenate([jnp.where(low, value, zero), jnp.where(low, zero, value)], axis=0)


def pick_heads(value):
    rows = value.shape[0] // 2
    upper, lower = value[:rows], value[rows:]
    return jnp.where(head_masks(upper.shape), upper, lower)


def causal_pair():
    row = lax.broadcasted_iota(jnp.int32, (SPAN, 2 * SPAN), 0)
    col = lax.broadcasted_iota(jnp.int32, (SPAN, 2 * SPAN), 1)
    return row >= jnp.where(col >= SPAN, col - SPAN, col)


def same_head(value):
    row = lax.broadcasted_iota(jnp.int32, value.shape, 0)
    col = lax.broadcasted_iota(jnp.int32, value.shape, 1)
    return jnp.where((row < HEAD) == (col < HEAD), value, jnp.zeros_like(value))


def to_blocks(value):
    return value.reshape(-1, SEQ // BLOCK, BLOCK, HEADS, HEAD)


def plain_local(tokens, w_query, w_key, w_value, w_gate, w_out, w_one, w_two, w_three, cotangent):
    axes = ("dp", "fsdp")
    rows, width = w_query.shape
    hidden = w_one.shape[1]
    attn_all = lax.all_gather(
        jnp.concatenate((w_query, w_key, w_value, w_gate, w_out), axis=1), axes, axis=0, tiled=True
    )
    ffn_all = lax.all_gather(
        jnp.concatenate((w_one, w_two, w_three.reshape(rows, hidden)), axis=1),
        axes,
        axis=0,
        tiled=True,
    )
    wq, wk, wv, wu, wo = (attn_all[:, i * width : (i + 1) * width] for i in range(5))
    w1 = ffn_all[:, :hidden]
    w2 = ffn_all[:, hidden : 2 * hidden]
    w3 = ffn_all[:, 2 * hidden :].reshape(hidden, width)
    x = tokens.astype(jnp.float32)
    scale_one = row_scale(x)
    normed = (x * scale_one).astype(jnp.bfloat16)
    pre_q = matmul(normed, wq)
    pre_k = matmul(normed, wk)
    pre_v = matmul(normed, wv)
    pre_u = matmul(normed, wu)
    q_blocks = to_blocks((pre_q * logistic(pre_q)).astype(jnp.bfloat16))
    k_blocks = to_blocks((pre_k * logistic(pre_k)).astype(jnp.bfloat16))
    v_blocks = to_blocks(pre_v.astype(jnp.bfloat16))
    causal = jnp.tril(jnp.ones((BLOCK, BLOCK), jnp.float32))
    scores = (
        jnp.einsum("bnchd,bnehd->bnhce", q_blocks, k_blocks, preferred_element_type=jnp.float32)
        * causal
    ).astype(jnp.bfloat16)
    inner = jnp.einsum("bnhce,bnehd->bnchd", scores, v_blocks, preferred_element_type=jnp.float32)
    block_kv = jnp.einsum(
        "bnchd,bnche->bnhde", k_blocks, v_blocks, preferred_element_type=jnp.float32
    )
    state = (jnp.cumsum(block_kv, axis=1) - block_kv).astype(jnp.bfloat16)
    outer = jnp.einsum("bnchd,bnhde->bnche", q_blocks, state, preferred_element_type=jnp.float32)
    attn = (inner + outer).reshape(x.shape)
    scale_two = row_scale(attn)
    attn_normed = attn * scale_two
    sig = logistic(pre_u)
    gated = (attn_normed * sig).astype(jnp.bfloat16)
    mid = x + matmul(gated, wo)
    scale_three = row_scale(mid)
    normed_two = (mid * scale_three).astype(jnp.bfloat16)
    first = matmul(normed_two, w1)
    second = matmul(normed_two, w2)
    product = (first * second).astype(jnp.bfloat16)
    output = (mid + matmul(product, w3)).astype(jnp.bfloat16)
    grad_three = weight_grad(product, cotangent)
    dprod = matmul_tr(cotangent, w3)
    d_first = (dprod * second).astype(jnp.bfloat16)
    d_second = (dprod * first).astype(jnp.bfloat16)
    grad_one = weight_grad(normed_two, d_first)
    grad_two = weight_grad(normed_two, d_second)
    d_normed_two = matmul_tr(d_first, w1) + matmul_tr(d_second, w2)
    d_mid = cotangent.astype(jnp.float32) + scale_back(mid, scale_three, d_normed_two)
    d_branch = d_mid.astype(jnp.bfloat16)
    grad_out = weight_grad(gated, d_branch)
    d_gated = matmul_tr(d_branch, wo)
    d_pre_u = (d_gated * attn_normed * sig * (1.0 - sig)).astype(jnp.bfloat16)
    d_attn = scale_back(attn, scale_two, d_gated * sig).astype(jnp.bfloat16)
    d_blocks = to_blocks(d_attn)
    d_scores = (
        jnp.einsum("bnchd,bnehd->bnhce", d_blocks, v_blocks, preferred_element_type=jnp.float32)
        * causal
    ).astype(jnp.bfloat16)
    d_state = jnp.einsum(
        "bnchd,bnche->bnhde", q_blocks, d_blocks, preferred_element_type=jnp.float32
    )
    d_kv = (lax.cumsum(d_state, axis=1, reverse=True) - d_state).astype(jnp.bfloat16)
    dq_full = jnp.einsum(
        "bnhce,bnehd->bnchd", d_scores, k_blocks, preferred_element_type=jnp.float32
    ) + jnp.einsum("bnche,bnhde->bnchd", d_blocks, state, preferred_element_type=jnp.float32)
    dk_full = jnp.einsum(
        "bnhce,bnchd->bnehd", d_scores, q_blocks, preferred_element_type=jnp.float32
    ) + jnp.einsum("bnche,bnhde->bnchd", v_blocks, d_kv, preferred_element_type=jnp.float32)
    dv_full = jnp.einsum(
        "bnhce,bnchd->bnehd", scores, d_blocks, preferred_element_type=jnp.float32
    ) + jnp.einsum("bnchd,bnhde->bnche", k_blocks, d_kv, preferred_element_type=jnp.float32)
    d_query = (dq_full.reshape(x.shape) * swish_slope(pre_q)).astype(jnp.bfloat16)
    d_key = (dk_full.reshape(x.shape) * swish_slope(pre_k)).astype(jnp.bfloat16)
    d_value = dv_full.reshape(x.shape).astype(jnp.bfloat16)
    grad_query = weight_grad(normed, d_query)
    grad_key = weight_grad(normed, d_key)
    grad_value = weight_grad(normed, d_value)
    grad_gate = weight_grad(normed, d_pre_u)
    d_normed = (
        matmul_tr(d_query, wq)
        + matmul_tr(d_key, wk)
        + matmul_tr(d_value, wv)
        + matmul_tr(d_pre_u, wu)
    )
    grad_tokens = (d_mid + scale_back(x, scale_one, d_normed)).astype(jnp.bfloat16)
    half = jnp.bfloat16
    ffn_grads = jnp.concatenate(
        (
            grad_one.astype(half),
            grad_two.astype(half),
            grad_three.astype(half).reshape(width, hidden),
        ),
        axis=1,
    )
    attn_grads = jnp.concatenate(
        [g.astype(half) for g in (grad_query, grad_key, grad_value, grad_gate, grad_out)], axis=1
    )
    ffn_sum = lax.psum_scatter(ffn_grads, axes, scatter_dimension=0, tiled=True)
    attn_sum = lax.psum_scatter(attn_grads, axes, scatter_dimension=0, tiled=True)
    ffn_sum = ffn_sum.astype(jnp.float32)
    attn_sum = attn_sum.astype(jnp.float32)
    shares = tuple(attn_sum[:, i * width : (i + 1) * width] for i in range(5)) + (
        ffn_sum[:, :hidden],
        ffn_sum[:, hidden : 2 * hidden],
        ffn_sum[:, 2 * hidden :].reshape(w_three.shape),
    )
    return (
        output,
        grad_tokens,
        shares[0],
        shares[1],
        shares[2],
        shares[3],
        shares[4],
        shares[5],
        shares[6],
        shares[7],
    )


class Copies:
    def __init__(self, sems):
        self.sems, self.count = sems, 0

    def start(self, src, dst):
        copy = pltpu.make_async_copy(src, dst, self.sems.at[self.count])
        self.count += 1
        copy.start()
        return copy


def forward_chunks(width, hidden):
    chunks = []
    for t in range(5):
        chunks += [(t, c, width // 2) for c in range(0, width, width // 2)]
    for c in range(0, hidden, width):
        size = min(width, hidden - c)
        chunks += [(5, c, size), (6, c, size)]
    chunks += [(7, c, 256) for c in range(0, width, 256)]
    return chunks


SLOTS, SLOTS3, SPACING = 5, 3, 2
ACTS = ("nrm", "q", "sq", "k", "sk", "v", "sig", "att", "y", "mid", "n2", "g1", "g2", "prod", "out")


def forward_kernel(cube, chunks, *refs):
    tok, shards = refs[0], refs[1:9]
    weights = refs[9:17]
    acts = dict(zip(ACTS, refs[17 : 17 + len(ACTS)]))
    (nb, ab, sb, a1, a2, a3, fu, fa, fm, stage, stage3, send, recv, own, local) = refs[17 + len(ACTS) :]
    cube.place()
    core, k, n = cube.bits[0], cube.k, len(chunks)
    width = tok.shape[1]
    mine = []
    for t in range(8):
        mine.append(pltpu.make_async_copy(shards[t], weights[t].at[cube.at(())], own.at[t]))
        mine[-1].start()
    cube.barrier()
    copies = Copies(local)


    def copy(c, s, v):
        t, c0, w = chunks[c]
        order = cube.kinds[c % 2][v]
        where = cube.at(order[:s]) + (slice(None), pl.ds(c0, w))
        src = shards[t].at[:, pl.ds(c0, w)] if s == 0 else weights[t].at[where]
        return pltpu.make_async_remote_copy(
            src_ref=src,
            dst_ref=weights[t].at[where],
            send_sem=send.at[c, s],
            recv_sem=recv.at[c, s],
            device_id=cube.partner(order[s]),
            device_id_type=MESH,
        )

    def both(c, s, act):
        first, second = cube.kinds[c % 2]
        if first[s] == second[s] and set(first[:s]) == set(second[:s]):
            act(copy(c, s, 0))
        else:

            @pl.when(core == 0)
            def _():
                act(copy(c, s, 0))

            @pl.when(core == 1)
            def _():
                act(copy(c, s, 1))


    whole = (slice(None),) * (k + 1)
    pending = {}

    def out_of(name, src):
        pending[name] = copies.start(src, acts[name])

    def settle(*names):
        for name in names:
            if name in pending:
                pending.pop(name).wait()

    def cols(ref, c, w):
        return ref[whole + (pl.ds(pl.multiple_of(c, 256), w),)].reshape(-1, w)

    def tiles(total, body):
        def step(i, carry):
            body(i // 2, i % 2)
            return carry

        lax.fori_loop(0, total // 256 * 2, step, 0)

    def rows(body, size=128):
        def step(i, carry):
            body(at_row(i, size))
            return carry

        lax.fori_loop(0, SEQ // size, step, 0)

    def norm_one():
        def body(r):
            x = tok[r, :].astype(F32)
            nb[r, :] = (x * row_scale(x)).astype(BF16)

        rows(body)
        out_of("nrm", nb)

    def project(t, c0, w, ref):
        def body(j, h):
            r = at_row(h, 512)
            to = pl.ds(pl.multiple_of(c0 + j * 256, 256), 256)
            acc = matmul(nb[r, :], cols(ref, j * 256, 256))
            if t == 3:
                fu[r, to] = acc
            elif t == 2:
                a3[r, to] = acc.astype(BF16)
            else:
                slope_to = pl.ds(pl.multiple_of(width + c0 + j * 256, 256), 256)
                sig = logistic(acc)
                dst = a1 if t == 0 else a2
                dst[r, to] = (acc * sig).astype(BF16)
                dst[r, slope_to] = (sig * (1.0 + acc * (1.0 - sig))).astype(BF16)

        tiles(w, body)
        if c0 + w == width:
            if t == 2:
                out_of("v", a3.at[:, pl.ds(0, width)])
            elif t < 2:
                src = a1 if t == 0 else a2
                out_of("qk"[t], src.at[:, pl.ds(0, width)])
                out_of(("sq", "sk")[t], src.at[:, pl.ds(width, width)])

    def attend(first, last):
        mask = causal_pair()

        def pair(p, carry):
            at = pl.ds(pl.multiple_of(p * 128, 128), 128)
            state = jnp.zeros((128, 128), F32)
            for b in range(SEQ // SPAN):
                r = pl.ds(b * SPAN, SPAN)
                q, kk, v = a1[r, at], a2[r, at], a3[r, at]
                scores = jnp.where(mask, matmul_tr(q, two_heads(kk)), 0.0).astype(BF16)
                acc = matmul(scores, two_heads(v))
                if b > 0:
                    acc += matmul(q, state.astype(BF16))
                fa[r, at] = acc
                if b + 1 < SEQ // SPAN:
                    state += same_head(weight_grad(kk, v))
            return carry

        lax.fori_loop(first, last, pair, 0)
    def gate():
        def body(r):
            attn, sig = fa[r, :], logistic(fu[r, :])
            a3[r, pl.ds(width, width)] = (attn * row_scale(attn) * sig).astype(BF16)
            ab[r, :] = attn.astype(BF16)
            sb[r, :] = sig.astype(BF16)

        rows(body)
        out_of("att", ab)
        out_of("sig", sb)
        out_of("y", a3.at[:, pl.ds(width, width)])

    def project_out(c0, w, ref):
        def body(j, h):
            r = at_row(h, 512)
            to = pl.ds(pl.multiple_of(c0 + j * 256, 256), 256)
            fm[r, to] = tok[r, to].astype(F32) + matmul(
                a3[r, pl.ds(width, width)], cols(ref, j * 256, 256)
            )

        tiles(w, body)

    def norm_two():
        settle("nrm")

        def body(r):
            mid = fm[r, :]
            nb[r, :] = (mid * row_scale(mid)).astype(BF16)

        rows(body)
        out_of("mid", fm)
        out_of("n2", nb)
        settle("q", "sq", "k", "sk", "v", "y")

    def hidden(c0, w, one, two):
        def body(j, h):
            r = at_row(h, 512)
            to = pl.ds(pl.multiple_of(c0 + j * 256, 256), 256)
            first = matmul(nb[r, :], cols(one, j * 256, 256))
            second = matmul(nb[r, :], cols(two, j * 256, 256))
            a1[r, to] = first.astype(BF16)
            a2[r, to] = second.astype(BF16)
            a3[r, to] = (first * second).astype(BF16)

        tiles(w, body)
        if c0 + w == a1.shape[1]:
            out_of("g1", a1)
            out_of("g2", a2)
            out_of("prod", a3)
            settle("n2")

    def down(c0, w, ref):
        def body(j, h):
            r = at_row(h, 512)
            to = pl.ds(pl.multiple_of(c0 + j * 256, 256), 256)
            nb[r, to] = (fm[r, to] + matmul(a3[r, :], cols(ref, j * 256, 256))).astype(BF16)

        tiles(w, body)
        if c0 + w == width:
            out_of("out", nb)

    index = {(t, c0): i for i, (t, c0, w) in enumerate(chunks)}
    items = [((), norm_one)]
    for i, (t, c0, w) in enumerate(chunks):
        last = c0 + w == width
        if t < 4:
            items.append(((i,), functools.partial(project, t, c0, w)))
            if t == 2 and last:
                items += [((), functools.partial(attend, 0, 4)), ((), functools.partial(attend, 4, 8))]
            if t == 3 and last:
                items.append(((), gate))
        elif t == 4:
            items.append(((i,), functools.partial(project_out, c0, w)))
            if last:
                items.append(((), norm_two))
        elif t == 5:
            items.append(((i, index[6, c0]), functools.partial(hidden, c0, w)))
        elif t == 7:
            items.append(((i,), functools.partial(down, c0, w)))

    free = {False: list(range(SLOTS)), True: list(range(SLOTS3))}
    arrived, staged = [], {}

    def stage_some(tick):
        while arrived and free[chunks[arrived[0]][0] == 7]:
            c = arrived.pop(0)
            t, c0, w = chunks[c]
            slot = free[t == 7].pop(0)
            dst = (stage3 if t == 7 else stage).at[(slot,) + whole + (pl.ds(0, w),)]
            cp = copies.start(weights[t].at[whole + (pl.ds(c0, w),)], dst)
            staged[c] = (tick, slot, cp)

    def run(tick, budget):
        while items and budget > 0:
            needs, act = items[0]
            if any(c not in staged or staged[c][0] >= tick for c in needs):
                return
            items.pop(0)
            given = []
            for c in needs:
                _, slot, cp = staged[c]
                cp.wait()
                given.append((stage3 if chunks[c][0] == 7 else stage).at[slot])
            act(*given)
            for c in needs:
                free[chunks[c][0] == 7].append(staged[c][1])
            budget -= 1

    settled = set()
    ticks = n + k * SPACING
    for tick in range(ticks):
        for c in range(n):
            d = tick - c
            if d < 0 or d % SPACING or d // SPACING > k:
                continue
            s = d // SPACING
            if s > 0:
                both(c, s - 1, lambda cp: cp.wait_recv())
            if s == 1 and chunks[c][0] not in settled:
                settled.add(chunks[c][0])
                mine[chunks[c][0]].wait()
            if s < k:
                both(c, s, lambda cp: cp.start())
            else:
                arrived.append(c)
        run(tick, 2)
        stage_some(tick)
    tick = ticks
    while items:
        run(tick, 1)
        stage_some(tick)
        tick += 1
    for c in range(n):
        for s in range(k):
            both(c, s, lambda cp: cp.wait_send())
    settle(*list(pending))


def forward(cube, tokens, shards):
    width, hidden = tokens.shape[1], shards[5].shape[1]
    chunks = forward_chunks(width, hidden)
    n, k = len(chunks), cube.k
    cubed = (2,) * k
    act = lambda dtype: jax.ShapeDtypeStruct(tokens.shape, dtype)
    kinds = {"mid": act(F32)}
    kinds.update(dict.fromkeys(("g1", "g2", "prod"), jax.ShapeDtypeStruct((SEQ, hidden), BF16)))
    outs = [jax.ShapeDtypeStruct(cubed + s.shape, s.dtype) for s in shards]
    outs += [kinds.get(name, act(BF16)) for name in ACTS]
    got = pl.pallas_call(
        functools.partial(forward_kernel, cube, chunks),
        out_shape=tuple(outs),
        in_specs=[pl.BlockSpec(memory_space=pltpu.VMEM)] * 9,
        out_specs=tuple([pl.BlockSpec(memory_space=pl.ANY)] * len(outs)),
        scratch_shapes=[
            pltpu.VMEM(tokens.shape, BF16),
            pltpu.VMEM(tokens.shape, BF16),
            pltpu.VMEM(tokens.shape, BF16),
            pltpu.VMEM((SEQ, hidden), BF16),
            pltpu.VMEM((SEQ, hidden), BF16),
            pltpu.VMEM((SEQ, hidden), BF16),
            pltpu.VMEM(tokens.shape, F32),
            pltpu.VMEM(tokens.shape, F32),
            pltpu.VMEM(tokens.shape, F32),
            pltpu.VMEM((SLOTS,) + cubed + (shards[0].shape[0], width), BF16),
            pltpu.VMEM((SLOTS3,) + cubed + (shards[7].shape[0], 256), BF16),
            pltpu.SemaphoreType.DMA((n, k)),
            pltpu.SemaphoreType.DMA((n, k)),
            pltpu.SemaphoreType.DMA((8,)),
            pltpu.SemaphoreType.DMA((n + len(ACTS),)),
        ],
        compiler_params=pltpu.CompilerParams(
            collective_id=0, has_side_effects=True, vmem_limit_bytes=64 * 1024 * 1024 - 65536
        ),
        name="gather_and_forward",
    )(tokens, *shards)
    return got[:8], dict(zip(ACTS, got[8:]))


KEPT = ("nrm", "q", "sq", "k", "sk", "v", "sig", "att", "y", "mid", "n2", "g1", "g2", "prod")
RING, PARTS, PARTS3, TILES, WIDE, WORK = 6, 3, 2, 4, 3, 4.0


def backward_chunks(width, hidden):
    chunks = [(7, c, 256) for c in range(0, width, 256)]
    for c in range(0, hidden, 512):
        size = min(512, hidden - c)
        chunks += [(5, c, size), (6, c, size)]
    chunks += [(t, c, 512) for t in (4, 3) for c in range(0, width, 512)]
    chunks += [(t, c, 512) for c in range(0, width, 512) for t in (0, 1, 2)]
    return chunks


class Tiles:
    def __init__(self, copies, ring, sources):
        self.copies, self.ring, self.sources = copies, ring, list(sources)
        self.slots, self.begun, self.used = ring.shape[0], [], 0
        self.fill()

    def fill(self):
        while len(self.begun) < min(len(self.sources), self.used + self.slots):
            i = len(self.begun)
            self.begun.append(self.copies.start(self.sources[i], self.ring.at[i % self.slots]))

    def take(self, act):
        i = self.used
        self.begun[i].wait()
        act(self.ring.at[i % self.slots])
        self.used += 1
        self.fill()


def backward_kernel(cube, chunks, *refs):
    cot, tok, weights = refs[0], refs[1], refs[2:10]
    acts = dict(zip(KEPT, refs[10 : 10 + len(KEPT)]))
    refs = refs[10 + len(KEPT) :]
    grad_tok, grads = refs[0], refs[1:9]
    a1, a2, a3, e0, e1, e2, nb, f1, f2, tiles, wide, part, part3, send, recv, local = refs[9:25]
    k, n = cube.k, len(chunks)
    landed = {False: refs[25 : 25 + k], True: refs[25 + k :]}
    cube.place()
    core = cube.bits[0]
    width, hidden = tok.shape[1], a1.shape[1]
    low, high = pl.ds(0, width), pl.ds(width, width)
    copies, loads = Copies(local), {}

    def load(name, dst, src=None):
        loads[name] = copies.start(acts[name] if src is None else src, dst)

    def need(*names):
        for name in names:
            if name in loads:
                loads.pop(name).wait()

    def rows_of(t, i):
        return weights[t].at[pl.ds(i * 256, 256), :]

    load("prod", a3)
    load("cot", e0, cot)
    blocks = width // 256
    order = [(7, i) for i in range(hidden // 256)] + [(4, i) for i in range(blocks)]
    order += [(t, i) for i in range(blocks) for t in range(4)]
    narrow = Tiles(copies, tiles, [rows_of(t, i) for t, i in order])
    load("g2", a2)
    load("g1", a1)
    load("n2", nb)
    broad = Tiles(copies, wide, [rows_of(t, i) for i in range(blocks) for t in (5, 6)])
    load("mid", f2)
    load("sig", e1)
    load("sk", e2)
    cube.barrier()


    def tall(c):
        return chunks[c][0] == 7

    place = {}
    for c in range(n):
        place[c] = sum(tall(b) == tall(c) for b in range(c))

    def held(c, s, v, own):
        o = cube.kinds[c % 2][v][::-1]
        bit = cube.bits[o[s]] if own else 1 - cube.bits[o[s]]
        where = tuple(bit if b == o[s] else slice(None) for b in range(k - 1, -1, -1) if b not in o[:s])
        if s == 0:
            return (part3, (place[c] % PARTS3,) + where) if tall(c) else (part, (place[c] % PARTS,) + where)
        ref = landed[tall(c)][s - 1]
        return ref, (place[c] % ref.shape[0],) + where

    def arrival(c, s):
        ref = landed[tall(c)][s]
        return ref, (place[c] % ref.shape[0],) + (slice(None),) * (k - 1 - s)

    def copy(c, s, v):
        cols = (slice(None), pl.ds(0, chunks[c][2]))
        src, where = held(c, s, v, False)
        dst, there = arrival(c, s)
        return pltpu.make_async_remote_copy(
            src_ref=src.at[where + cols],
            dst_ref=dst.at[there + cols],
            send_sem=send.at[c, s],
            recv_sem=recv.at[c, s],
            device_id=cube.partner(cube.kinds[c % 2][v][::-1][s]),
            device_id_type=MESH,
        )

    def begin(c, s, v):
        copy(c, s, v).start()

    def finish(c, s, v):
        cp = copy(c, s, v)
        cp.wait_recv()
        cp.wait_send()
        t, c0, w = chunks[c]
        mine, where = held(c, s, v, True)
        into, there = arrival(c, s)

        def body(j, carry):
            cols = (slice(None), pl.ds(pl.multiple_of(j * 128, 128), 128))
            left, right = mine[where + cols], into[there + cols]
            if s == k - 1:
                to = pl.ds(pl.multiple_of(c0 + j * 128, 128), 128)
                grads[t][:, to] = left.astype(F32) + right.astype(F32)
            else:
                into[there + cols] = left + right
            return carry

        lax.fori_loop(0, w // 128, body, 0)

    def both(c, s, act):
        first, second = (o[::-1] for o in cube.kinds[c % 2])
        if first[s] == second[s] and set(first[:s]) == set(second[:s]):
            act(c, s, 0)
        else:

            @pl.when(core == 0)
            def _():
                act(c, s, 0)

            @pl.when(core == 1)
            def _():
                act(c, s, 1)


    def halves(count, body):
        def step(i, carry):
            body(i // 2, at_row(i % 2, 512))
            return carry

        lax.fori_loop(0, count * 2, step, 0)

    def rows(body):
        def step(i, carry):
            body(at_row(i, 128))
            return carry

        lax.fori_loop(0, SEQ // 128, step, 0)

    def product_grad(c):
        need("prod", "cot")
        _, c0, w = chunks[c]
        slot = place[c] % PARTS3

        def step(x, carry):
            left = a3[:, pl.ds(pl.multiple_of(x * (hidden // 2), 128), hidden // 2)]
            got = weight_grad(left, e0[:, pl.ds(c0, w)])
            got = got.reshape((2,) * (k - 1) + (-1, w)).astype(BF16)
            part3[(slot, x) + (slice(None),) * (k + 1)] = got
            return carry

        lax.fori_loop(0, 2, step, 0)

    def grad(c, names, left, lefts, right, rights):
        need(*names)
        _, c0, w = chunks[c]
        slot = place[c] % PARTS

        def step(i, carry):
            j, h = i // 2, i % 2
            at = pl.ds(pl.multiple_of(lefts + h * (width // 2), 128), width // 2)
            to = pl.ds(pl.multiple_of(rights + c0 + j * 256, 128), 256)
            got = weight_grad(left[:, at], right[:, to])
            got = got.reshape((2,) * (k - 1) + (-1, 256)).astype(BF16)
            dst = pl.ds(pl.multiple_of(j * 256, 128), 256)
            part[(slot, h) + (slice(None),) * k + (dst,)] = got
            return carry

        lax.fori_loop(0, w // 256 * 2, step, 0)

    def product_back(i):
        need("g1", "g2")
        to = pl.ds(i * 256, 256)

        def act(tile):
            def body(_, r):
                back = matmul_tr(e0[r, :], tile[...])
                one, two = a1[r, to].astype(F32), a2[r, to].astype(F32)
                a1[r, to] = (back * two).astype(BF16)
                a2[r, to] = (back * one).astype(BF16)

            halves(1, body)

        narrow.take(act)

    def hidden_back(i):
        to = pl.ds(i * 256, 256)

        def first(tile):
            def body(_, r):
                f1[r, to] = matmul_tr(a1[r, :], tile[...])

            halves(1, body)

        def second(tile):
            def body(_, r):
                f1[r, to] += matmul_tr(a2[r, :], tile[...])

            halves(1, body)

        broad.take(first)
        broad.take(second)

    def mid_back():
        need("mid")

        def body(r):
            mid = f2[r, :]
            back = e0[r, :].astype(F32) + scale_back(mid, row_scale(mid), f1[r, :])
            f1[r, :] = back
            e0[r, :] = back.astype(BF16)

        rows(body)

    def out_back(i):
        to = pl.ds(i * 256, 256)

        def act(tile):
            def body(_, r):
                f2[r, to] = matmul_tr(e0[r, :], tile[...])

            halves(1, body)

        narrow.take(act)

    def gate_back():
        need("att", "sig")

        def body(r):
            back, attn, sig = f2[r, :], a3[r, high].astype(F32), e1[r, :].astype(F32)
            scale = row_scale(attn)
            e1[r, :] = (back * (attn * scale) * sig * (1.0 - sig)).astype(BF16)
            a3[r, high] = scale_back(attn, scale, back * sig).astype(BF16)

        rows(body)

    def attend_back(first, last):
        need("q", "k", "v", "sq", "sk")
        mask = causal_pair()
        count = SEQ // SPAN

        def pair(p, carry):
            at = pl.ds(pl.multiple_of(p * 128, 128), 128)
            up = pl.ds(pl.multiple_of(width + p * 128, 128), 128)
            state, states = jnp.zeros((128, 128), F32), [None]
            for b in range(count - 1):
                r = pl.ds(b * SPAN, SPAN)
                state += same_head(weight_grad(a1[r, up], a2[r, at]))
                states.append(state.astype(BF16))
            later = jnp.zeros((128, 128), F32)
            for b in reversed(range(count)):
                r = pl.ds(b * SPAN, SPAN)
                q, kk, v, d = a1[r, at], a1[r, up], a2[r, at], a3[r, up]
                keys = two_heads(kk)
                scores = jnp.where(mask, matmul_tr(q, keys), 0.0).astype(BF16)
                d_scores = jnp.where(mask, matmul_tr(d, two_heads(v)), 0.0).astype(BF16)
                dq = matmul(d_scores, keys)
                dk = pick_heads(weight_grad(d_scores, q))
                dv = pick_heads(weight_grad(scores, d))
                if b > 0:
                    dq += matmul_tr(d, states[b])
                if b + 1 < count:
                    d_kv = later.astype(BF16)
                    dk += matmul_tr(v, d_kv)
                    dv += matmul(kk, d_kv)
                if b > 0:
                    later += same_head(weight_grad(q, d))
                a1[r, at] = (dq * a2[r, up].astype(F32)).astype(BF16)
                a1[r, up] = (dk * e2[r, at].astype(F32)).astype(BF16)
                a2[r, at] = dv.astype(BF16)
            return carry

        lax.fori_loop(first, last, pair, 0)

    def normed_back(i):
        to = pl.ds(i * 256, 256)
        for t, (ref, cols) in enumerate(((a1, low), (a1, high), (a2, low), (e1, low))):

            def act(tile, t=t, ref=ref, cols=cols):
                def body(_, r):
                    got = matmul_tr(ref[r, cols], tile[...])
                    f2[r, to] = got if t == 0 else f2[r, to] + got

                halves(1, body)

            narrow.take(act)

    def token_back():
        need("tok")

        def body(r):
            x = e0[r, :].astype(F32)
            e0[r, :] = (f1[r, :] + scale_back(x, row_scale(x), f2[r, :])).astype(BF16)

        rows(body)
        load("end", grad_tok, e0)

    def after_product():
        load("y", a3.at[:, low])
        load("att", a3.at[:, high])

    def after_hidden():
        load("q", a1.at[:, low])
        load("k", a1.at[:, high])
        load("v", a2.at[:, low])
        load("sq", a2.at[:, high])
        load("nrm", nb)

    index = {(t, c0): c for c, (t, c0, w) in enumerate(chunks)}
    of = lambda *ts: [c for c in range(n) if chunks[c][0] in ts]
    items = [(("back", i), (), 1.1, functools.partial(product_back, i)) for i in range(hidden // 256)]
    items.append(("product", of(7), 0.0, after_product))
    items += [(("hidden", i), (), 3.8, functools.partial(hidden_back, i)) for i in range(blocks)]
    items.append(("mid", of(7), 3.0, mid_back))
    items += [(("out", i), (), 0.9, functools.partial(out_back, i)) for i in range(blocks)]
    items.append(("gate", (), 3.0, gate_back))
    items.append(("loads", of(5, 6), 0.0, after_hidden))
    items += [
        (("attend", i), (), 5.0, functools.partial(attend_back, 2 * i, 2 * i + 2))
        for i in range(width // 256)
    ]
    items.append(("tok", of(4), 0.0, lambda: load("tok", e0, tok)))
    items += [(("normed", i), (), 3.0, functools.partial(normed_back, i)) for i in range(blocks)]
    items.append(("tokens", (), 3.0, token_back))

    def make(c):
        t, c0, w = chunks[c]
        if t == 7:
            return (), functools.partial(product_grad, c)
        if t in (5, 6):
            after = [("back", i) for i in range((c0 + w) // 256)]
            return after, functools.partial(grad, c, ("n2",), nb, 0, (a1, a2)[t - 5], 0)
        if t == 4:
            return ("product", "mid"), functools.partial(grad, c, ("y",), a3, 0, e0, 0)
        if t == 3:
            return ("gate", "loads"), functools.partial(grad, c, ("nrm",), nb, 0, e1, 0)
        after = [("attend", i) for i in range((c0 + w) // 256)]
        right, at = ((a1, 0), (a1, width), (a2, 0))[t]
        return after, functools.partial(grad, c, ("nrm",), nb, 0, right, at)

    done, made, first, free = set(), 0, {}, set(range(n))
    tick = 0
    while items or made < n or any(tick <= first[c] + 2 * k for c in first):
        active = [(c, tick - first[c]) for c in sorted(first)]
        for c, d in active:
            if d > 0 and d % 2 == 0 and d <= 2 * k:
                both(c, d // 2 - 1, finish)
        for c, d in active:
            if d > 0 and d % 2 == 0 and d < 2 * k:
                both(c, d // 2, begin)
        if len(first) < made:
            c = len(first)
            first[c] = tick
            both(c, 0, begin)
        left = WORK

        def can_make():
            if made == n:
                return False
            busy = sum(
                tall(c) == tall(made) and not (c in first and tick >= first[c] + 2) for c in range(made)
            )
            return busy < (PARTS3 if tall(made) else PARTS) and all(x in done for x in make(made)[0])

        while left > 0:
            if can_make() and made - len(first) < 2:
                make(made)[1]()
                done.add(made)
                made += 1
                left -= 2.0
            elif items and all(x in done for x in items[0][1]):
                name, _, cost, act = items.pop(0)
                act()
                done.add(name)
                left -= cost
            else:
                break
        tick += 1
    need(*list(loads))


def backward(cube, tokens, weights, acts, cotangent):
    width, hidden = tokens.shape[1], weights[5].shape[1]
    chunks = backward_chunks(width, hidden)
    n, k = len(chunks), cube.k
    devices = 1 << k
    few, many = width // devices, hidden // devices
    landed = []
    for slots, count, cols in ((RING, few, 512), (width // 256, many, 256)):
        landed += [pltpu.VMEM((slots,) + (2,) * (k - 1 - s) + (count, cols), BF16) for s in range(k)]
    shapes = [(few, width)] * 5 + [(few, hidden)] * 2 + [(many, width)]
    outs = [jax.ShapeDtypeStruct(tokens.shape, BF16)] + [jax.ShapeDtypeStruct(s, F32) for s in shapes]
    square, broad = pltpu.VMEM(tokens.shape, BF16), pltpu.VMEM((SEQ, hidden), BF16)
    local_copies = len(KEPT) + 3 + hidden // 256 + 7 * (width // 256)
    return pl.pallas_call(
        functools.partial(backward_kernel, cube, chunks),
        out_shape=tuple(outs),
        in_specs=[pl.BlockSpec(memory_space=pl.ANY)] * (10 + len(KEPT)),
        out_specs=tuple(
            [pl.BlockSpec(memory_space=pl.ANY)] + [pl.BlockSpec(memory_space=pltpu.VMEM)] * 8
        ),
        scratch_shapes=[broad] * 3
        + [square] * 4
        + [pltpu.VMEM(tokens.shape, F32)] * 2
        + [
            pltpu.VMEM((TILES, 256, width), BF16),
            pltpu.VMEM((WIDE, 256, hidden), BF16),
            pltpu.VMEM((PARTS,) + (2,) * k + (few, 512), BF16),
            pltpu.VMEM((PARTS3,) + (2,) * k + (many, 256), BF16),
            pltpu.SemaphoreType.DMA((n, k)),
            pltpu.SemaphoreType.DMA((n, k)),
            pltpu.SemaphoreType.DMA((local_copies,)),
        ]
        + landed,
        compiler_params=pltpu.CompilerParams(
            collective_id=1, has_side_effects=True, vmem_limit_bytes=64 * 1024 * 1024 - 65536
        ),
        name="backward_and_sum",
    )(cotangent, tokens, *weights, *(acts[name] for name in KEPT))


def local(cube, tokens, w_query, w_key, w_value, w_gate, w_out, w_one, w_two, w_three, cotangent):
    shards = (w_query, w_key, w_value, w_gate, w_out, w_one, w_two, w_three)
    gathered, acts = forward(cube, tokens, shards)
    weights = [w.reshape(-1, w.shape[-1]) for w in gathered]
    return (acts["out"],) + tuple(backward(cube, tokens, weights, acts, cotangent))


def solution(mesh):
    nd, nf = mesh.shape["dp"], mesh.shape["fsdp"]
    rows = P(("dp", "fsdp"), None)

    def step(*args):
        fits = args[1].shape[0] % 16 == 0 and args[8].shape[0] % 8 == 0 and args[0].shape[0] == SEQ
        if fits:
            return local(Cube(nd, nf), *args)
        return plain_local(*args)

    return jax.shard_map(
        step, mesh=mesh, in_specs=(rows,) * 10, out_specs=(rows,) * 10, check_vma=False
    )
```

```python
import functools

import jax
import jax.numpy as jnp
from jax import lax
from jax.experimental import pallas as pl
from jax.experimental.pallas import tpu as pltpu
from jax.sharding import PartitionSpec as P

HEADS = 16
HEAD = 64
BLOCK = 128
SEQ = 1024
SPAN = 256
EPS = 1e-06
MESH = pl.DeviceIdType.MESH
F32 = jnp.float32
BF16 = jnp.bfloat16


def row_scale(value):
    return lax.rsqrt(jnp.mean(value * value, axis=-1, keepdims=True) + EPS)


def scale_back(value, scale, grad):
    return scale * grad - value * scale * scale * scale * jnp.mean(
        grad * value, axis=-1, keepdims=True
    )


def logistic(value):
    return 1.0 / (1.0 + jnp.exp(-value))


def swish_slope(value):
    sig = logistic(value)
    return sig * (1.0 + value * (1.0 - sig))


def matmul(left, right):
    return jnp.dot(left, right, preferred_element_type=jnp.float32)


def matmul_tr(left, right):
    return lax.dot_general(
        left, right, (((1,), (1,)), ((), ())), preferred_element_type=jnp.float32
    )


def weight_grad(left, right):
    return lax.dot_general(
        left, right, (((0,), (0,)), ((), ())), preferred_element_type=jnp.float32
    )


class Cube:
    def __init__(self, nd, nf):
        self.nd, self.nf = nd, nf
        self.kd, self.kf = nd.bit_length() - 1, nf.bit_length() - 1
        self.k = self.kd + self.kf
        top = [self.kf - 1, self.kf - 2]
        outer = list(range(self.kf, self.k))
        mid = list(range(self.kf - 3, 0, -1))
        self.kinds = (
            (top + outer + mid + [0], top + mid + outer + [0]),
            (outer + top + mid + [0], mid + top + outer + [0]),
        )

    def place(self):
        self.x, self.f = lax.axis_index("dp"), lax.axis_index("fsdp")
        index = self.x * self.nf + self.f
        self.bits = [(index // (1 << b)) % 2 for b in range(self.k)]

    def partner(self, b):
        step = 1 - 2 * self.bits[b]
        if b < self.kf:
            return (self.x, self.f + step * (1 << b))
        return (self.x + step * (1 << (b - self.kf)), self.f)

    def at(self, free, flip=None):
        return tuple(
            slice(None) if b in free else (1 - self.bits[b] if b == flip else self.bits[b])
            for b in range(self.k - 1, -1, -1)
        )

    def barrier(self):
        sem = pltpu.get_barrier_semaphore()
        for b in range(self.k):
            pl.semaphore_signal(sem, inc=1, device_id=self.partner(b), device_id_type=MESH)
        pl.semaphore_wait(sem, self.k)


def at_row(i, size):
    return pl.ds(pl.multiple_of(i * size, size), size)


def head_masks(shape):
    lane = lax.broadcasted_iota(jnp.int32, shape, len(shape) - 1)
    return lane < HEAD


def two_heads(value):
    low = head_masks(value.shape)
    zero = jnp.zeros_like(value)
    return jnp.concatenate([jnp.where(low, value, zero), jnp.where(low, zero, value)], axis=0)


def pick_heads(value):
    rows = value.shape[0] // 2
    upper, lower = value[:rows], value[rows:]
    return jnp.where(head_masks(upper.shape), upper, lower)


def causal_pair():
    row = lax.broadcasted_iota(jnp.int32, (SPAN, 2 * SPAN), 0)
    col = lax.broadcasted_iota(jnp.int32, (SPAN, 2 * SPAN), 1)
    return row >= jnp.where(col >= SPAN, col - SPAN, col)


def same_head(value):
    row = lax.broadcasted_iota(jnp.int32, value.shape, 0)
    col = lax.broadcasted_iota(jnp.int32, value.shape, 1)
    return jnp.where((row < HEAD) == (col < HEAD), value, jnp.zeros_like(value))


def to_blocks(value):
    return value.reshape(-1, SEQ // BLOCK, BLOCK, HEADS, HEAD)


def plain_local(tokens, w_query, w_key, w_value, w_gate, w_out, w_one, w_two, w_three, cotangent):
    axes = ("dp", "fsdp")
    rows, width = w_query.shape
    hidden = w_one.shape[1]
    attn_all = lax.all_gather(
        jnp.concatenate((w_query, w_key, w_value, w_gate, w_out), axis=1), axes, axis=0, tiled=True
    )
    ffn_all = lax.all_gather(
        jnp.concatenate((w_one, w_two, w_three.reshape(rows, hidden)), axis=1),
        axes,
        axis=0,
        tiled=True,
    )
    wq, wk, wv, wu, wo = (attn_all[:, i * width : (i + 1) * width] for i in range(5))
    w1 = ffn_all[:, :hidden]
    w2 = ffn_all[:, hidden : 2 * hidden]
    w3 = ffn_all[:, 2 * hidden :].reshape(hidden, width)
    x = tokens.astype(jnp.float32)
    scale_one = row_scale(x)
    normed = (x * scale_one).astype(jnp.bfloat16)
    pre_q = matmul(normed, wq)
    pre_k = matmul(normed, wk)
    pre_v = matmul(normed, wv)
    pre_u = matmul(normed, wu)
    q_blocks = to_blocks((pre_q * logistic(pre_q)).astype(jnp.bfloat16))
    k_blocks = to_blocks((pre_k * logistic(pre_k)).astype(jnp.bfloat16))
    v_blocks = to_blocks(pre_v.astype(jnp.bfloat16))
    causal = jnp.tril(jnp.ones((BLOCK, BLOCK), jnp.float32))
    scores = (
        jnp.einsum("bnchd,bnehd->bnhce", q_blocks, k_blocks, preferred_element_type=jnp.float32)
        * causal
    ).astype(jnp.bfloat16)
    inner = jnp.einsum("bnhce,bnehd->bnchd", scores, v_blocks, preferred_element_type=jnp.float32)
    block_kv = jnp.einsum(
        "bnchd,bnche->bnhde", k_blocks, v_blocks, preferred_element_type=jnp.float32
    )
    state = (jnp.cumsum(block_kv, axis=1) - block_kv).astype(jnp.bfloat16)
    outer = jnp.einsum("bnchd,bnhde->bnche", q_blocks, state, preferred_element_type=jnp.float32)
    attn = (inner + outer).reshape(x.shape)
    scale_two = row_scale(attn)
    attn_normed = attn * scale_two
    sig = logistic(pre_u)
    gated = (attn_normed * sig).astype(jnp.bfloat16)
    mid = x + matmul(gated, wo)
    scale_three = row_scale(mid)
    normed_two = (mid * scale_three).astype(jnp.bfloat16)
    first = matmul(normed_two, w1)
    second = matmul(normed_two, w2)
    product = (first * second).astype(jnp.bfloat16)
    output = (mid + matmul(product, w3)).astype(jnp.bfloat16)
    grad_three = weight_grad(product, cotangent)
    dprod = matmul_tr(cotangent, w3)
    d_first = (dprod * second).astype(jnp.bfloat16)
    d_second = (dprod * first).astype(jnp.bfloat16)
    grad_one = weight_grad(normed_two, d_first)
    grad_two = weight_grad(normed_two, d_second)
    d_normed_two = matmul_tr(d_first, w1) + matmul_tr(d_second, w2)
    d_mid = cotangent.astype(jnp.float32) + scale_back(mid, scale_three, d_normed_two)
    d_branch = d_mid.astype(jnp.bfloat16)
    grad_out = weight_grad(gated, d_branch)
    d_gated = matmul_tr(d_branch, wo)
    d_pre_u = (d_gated * attn_normed * sig * (1.0 - sig)).astype(jnp.bfloat16)
    d_attn = scale_back(attn, scale_two, d_gated * sig).astype(jnp.bfloat16)
    d_blocks = to_blocks(d_attn)
    d_scores = (
        jnp.einsum("bnchd,bnehd->bnhce", d_blocks, v_blocks, preferred_element_type=jnp.float32)
        * causal
    ).astype(jnp.bfloat16)
    d_state = jnp.einsum(
        "bnchd,bnche->bnhde", q_blocks, d_blocks, preferred_element_type=jnp.float32
    )
    d_kv = (lax.cumsum(d_state, axis=1, reverse=True) - d_state).astype(jnp.bfloat16)
    dq_full = jnp.einsum(
        "bnhce,bnehd->bnchd", d_scores, k_blocks, preferred_element_type=jnp.float32
    ) + jnp.einsum("bnche,bnhde->bnchd", d_blocks, state, preferred_element_type=jnp.float32)
    dk_full = jnp.einsum(
        "bnhce,bnchd->bnehd", d_scores, q_blocks, preferred_element_type=jnp.float32
    ) + jnp.einsum("bnche,bnhde->bnchd", v_blocks, d_kv, preferred_element_type=jnp.float32)
    dv_full = jnp.einsum(
        "bnhce,bnchd->bnehd", scores, d_blocks, preferred_element_type=jnp.float32
    ) + jnp.einsum("bnchd,bnhde->bnche", k_blocks, d_kv, preferred_element_type=jnp.float32)
    d_query = (dq_full.reshape(x.shape) * swish_slope(pre_q)).astype(jnp.bfloat16)
    d_key = (dk_full.reshape(x.shape) * swish_slope(pre_k)).astype(jnp.bfloat16)
    d_value = dv_full.reshape(x.shape).astype(jnp.bfloat16)
    grad_query = weight_grad(normed, d_query)
    grad_key = weight_grad(normed, d_key)
    grad_value = weight_grad(normed, d_value)
    grad_gate = weight_grad(normed, d_pre_u)
    d_normed = (
        matmul_tr(d_query, wq)
        + matmul_tr(d_key, wk)
        + matmul_tr(d_value, wv)
        + matmul_tr(d_pre_u, wu)
    )
    grad_tokens = (d_mid + scale_back(x, scale_one, d_normed)).astype(jnp.bfloat16)
    half = jnp.bfloat16
    ffn_grads = jnp.concatenate(
        (
            grad_one.astype(half),
            grad_two.astype(half),
            grad_three.astype(half).reshape(width, hidden),
        ),
        axis=1,
    )
    attn_grads = jnp.concatenate(
        [g.astype(half) for g in (grad_query, grad_key, grad_value, grad_gate, grad_out)], axis=1
    )
    ffn_sum = lax.psum_scatter(ffn_grads, axes, scatter_dimension=0, tiled=True)
    attn_sum = lax.psum_scatter(attn_grads, axes, scatter_dimension=0, tiled=True)
    ffn_sum = ffn_sum.astype(jnp.float32)
    attn_sum = attn_sum.astype(jnp.float32)
    shares = tuple(attn_sum[:, i * width : (i + 1) * width] for i in range(5)) + (
        ffn_sum[:, :hidden],
        ffn_sum[:, hidden : 2 * hidden],
        ffn_sum[:, 2 * hidden :].reshape(w_three.shape),
    )
    return (
        output,
        grad_tokens,
        shares[0],
        shares[1],
        shares[2],
        shares[3],
        shares[4],
        shares[5],
        shares[6],
        shares[7],
    )


class Copies:
    def __init__(self, sems):
        self.sems, self.count = sems, 0

    def start(self, src, dst):
        copy = pltpu.make_async_copy(src, dst, self.sems.at[self.count])
        self.count += 1
        copy.start()
        return copy


def forward_chunks(width, hidden):
    chunks = []
    for t in range(5):
        chunks += [(t, c, width // 2) for c in range(0, width, width // 2)]
    for c in range(0, hidden, width):
        size = min(width, hidden - c)
        chunks += [(5, c, size), (6, c, size)]
    chunks += [(7, c, 256) for c in range(0, width, 256)]
    return chunks


SLOTS, SLOTS3, SPACING = 5, 3, 2
ACTS = ("nrm", "q", "sq", "k", "sk", "v", "sig", "att", "y", "mid", "n2", "g1", "g2", "prod", "out")


def forward_kernel(cube, chunks, *refs):
    tok, shards = refs[0], refs[1:9]
    weights = refs[9:17]
    acts = dict(zip(ACTS, refs[17 : 17 + len(ACTS)]))
    (nb, ab, sb, a1, a2, a3, fu, fa, fm, stage, stage3, send, recv, own, local) = refs[17 + len(ACTS) :]
    cube.place()
    core, k, n = cube.bits[0], cube.k, len(chunks)
    width = tok.shape[1]
    mine = []
    for t in range(8):
        mine.append(pltpu.make_async_copy(shards[t], weights[t].at[cube.at(())], own.at[t]))
        mine[-1].start()
    cube.barrier()
    copies = Copies(local)


    def copy(c, s, v):
        t, c0, w = chunks[c]
        order = cube.kinds[c % 2][v]
        where = cube.at(order[:s]) + (slice(None), pl.ds(c0, w))
        src = shards[t].at[:, pl.ds(c0, w)] if s == 0 else weights[t].at[where]
        return pltpu.make_async_remote_copy(
            src_ref=src,
            dst_ref=weights[t].at[where],
            send_sem=send.at[c, s],
            recv_sem=recv.at[c, s],
            device_id=cube.partner(order[s]),
            device_id_type=MESH,
        )

    def both(c, s, act):
        first, second = cube.kinds[c % 2]
        if first[s] == second[s] and set(first[:s]) == set(second[:s]):
            act(copy(c, s, 0))
        else:

            @pl.when(core == 0)
            def _():
                act(copy(c, s, 0))

            @pl.when(core == 1)
            def _():
                act(copy(c, s, 1))


    whole = (slice(None),) * (k + 1)
    pending = {}

    def out_of(name, src):
        pending[name] = copies.start(src, acts[name])

    def settle(*names):
        for name in names:
            if name in pending:
                pending.pop(name).wait()

    def cols(ref, c, w):
        return ref[whole + (pl.ds(pl.multiple_of(c, 256), w),)].reshape(-1, w)

    def tiles(total, body):
        def step(i, carry):
            body(i // 2, i % 2)
            return carry

        lax.fori_loop(0, total // 256 * 2, step, 0)

    def rows(body, size=128):
        def step(i, carry):
            body(at_row(i, size))
            return carry

        lax.fori_loop(0, SEQ // size, step, 0)

    def norm_one():
        def body(r):
            x = tok[r, :].astype(F32)
            nb[r, :] = (x * row_scale(x)).astype(BF16)

        rows(body)
        out_of("nrm", nb)

    def project(t, c0, w, ref):
        def body(j, h):
            r = at_row(h, 512)
            to = pl.ds(pl.multiple_of(c0 + j * 256, 256), 256)
            acc = matmul(nb[r, :], cols(ref, j * 256, 256))
            if t == 3:
                fu[r, to] = acc
            elif t == 2:
                a3[r, to] = acc.astype(BF16)
            else:
                slope_to = pl.ds(pl.multiple_of(width + c0 + j * 256, 256), 256)
                sig = logistic(acc)
                dst = a1 if t == 0 else a2
                dst[r, to] = (acc * sig).astype(BF16)
                dst[r, slope_to] = (sig * (1.0 + acc * (1.0 - sig))).astype(BF16)

        tiles(w, body)
        if c0 + w == width:
            if t == 2:
                out_of("v", a3.at[:, pl.ds(0, width)])
            elif t < 2:
                src = a1 if t == 0 else a2
                out_of("qk"[t], src.at[:, pl.ds(0, width)])
                out_of(("sq", "sk")[t], src.at[:, pl.ds(width, width)])

    def attend(first, last):
        mask = causal_pair()

        def pair(p, carry):
            at = pl.ds(pl.multiple_of(p * 128, 128), 128)
            state = jnp.zeros((128, 128), F32)
            for b in range(SEQ // SPAN):
                r = pl.ds(b * SPAN, SPAN)
                q, kk, v = a1[r, at], a2[r, at], a3[r, at]
                scores = jnp.where(mask, matmul_tr(q, two_heads(kk)), 0.0).astype(BF16)
                acc = matmul(scores, two_heads(v))
                if b > 0:
                    acc += matmul(q, state.astype(BF16))
                fa[r, at] = acc
                if b + 1 < SEQ // SPAN:
                    state += same_head(weight_grad(kk, v))
            return carry

        lax.fori_loop(first, last, pair, 0)
    def gate():
        def body(r):
            attn, sig = fa[r, :], logistic(fu[r, :])
            a3[r, pl.ds(width, width)] = (attn * row_scale(attn) * sig).astype(BF16)
            ab[r, :] = attn.astype(BF16)
            sb[r, :] = sig.astype(BF16)

        rows(body)
        out_of("att", ab)
        out_of("sig", sb)
        out_of("y", a3.at[:, pl.ds(width, width)])

    def project_out(c0, w, ref):
        def body(j, h):
            r = at_row(h, 512)
            to = pl.ds(pl.multiple_of(c0 + j * 256, 256), 256)
            fm[r, to] = tok[r, to].astype(F32) + matmul(
                a3[r, pl.ds(width, width)], cols(ref, j * 256, 256)
            )

        tiles(w, body)

    def norm_two():
        settle("nrm")

        def body(r):
            mid = fm[r, :]
            nb[r, :] = (mid * row_scale(mid)).astype(BF16)

        rows(body)
        out_of("mid", fm)
        out_of("n2", nb)
        settle("q", "sq", "k", "sk", "v", "y")

    def hidden(c0, w, one, two):
        def body(j, h):
            r = at_row(h, 512)
            to = pl.ds(pl.multiple_of(c0 + j * 256, 256), 256)
            first = matmul(nb[r, :], cols(one, j * 256, 256))
            second = matmul(nb[r, :], cols(two, j * 256, 256))
            a1[r, to] = first.astype(BF16)
            a2[r, to] = second.astype(BF16)
            a3[r, to] = (first * second).astype(BF16)

        tiles(w, body)
        if c0 + w == a1.shape[1]:
            out_of("g1", a1)
            out_of("g2", a2)
            out_of("prod", a3)
            settle("n2")

    def down(c0, w, ref):
        def body(j, h):
            r = at_row(h, 512)
            to = pl.ds(pl.multiple_of(c0 + j * 256, 256), 256)
            nb[r, to] = (fm[r, to] + matmul(a3[r, :], cols(ref, j * 256, 256))).astype(BF16)

        tiles(w, body)
        if c0 + w == width:
            out_of("out", nb)

    index = {(t, c0): i for i, (t, c0, w) in enumerate(chunks)}
    items = [((), norm_one)]
    for i, (t, c0, w) in enumerate(chunks):
        last = c0 + w == width
        if t < 4:
            items.append(((i,), functools.partial(project, t, c0, w)))
            if t == 2 and last:
                items += [((), functools.partial(attend, 0, 4)), ((), functools.partial(attend, 4, 8))]
            if t == 3 and last:
                items.append(((), gate))
        elif t == 4:
            items.append(((i,), functools.partial(project_out, c0, w)))
            if last:
                items.append(((), norm_two))
        elif t == 5:
            items.append(((i, index[6, c0]), functools.partial(hidden, c0, w)))
        elif t == 7:
            items.append(((i,), functools.partial(down, c0, w)))

    free = {False: list(range(SLOTS)), True: list(range(SLOTS3))}
    arrived, staged = [], {}

    def stage_some(tick):
        while arrived and free[chunks[arrived[0]][0] == 7]:
            c = arrived.pop(0)
            t, c0, w = chunks[c]
            slot = free[t == 7].pop(0)
            dst = (stage3 if t == 7 else stage).at[(slot,) + whole + (pl.ds(0, w),)]
            cp = copies.start(weights[t].at[whole + (pl.ds(c0, w),)], dst)
            staged[c] = (tick, slot, cp)

    def run(tick, budget):
        while items and budget > 0:
            needs, act = items[0]
            if any(c not in staged or staged[c][0] >= tick for c in needs):
                return
            items.pop(0)
            given = []
            for c in needs:
                _, slot, cp = staged[c]
                cp.wait()
                given.append((stage3 if chunks[c][0] == 7 else stage).at[slot])
            act(*given)
            for c in needs:
                free[chunks[c][0] == 7].append(staged[c][1])
            budget -= 1

    settled = set()
    ticks = n + k * SPACING
    for tick in range(ticks):
        for c in range(n):
            d = tick - c
            if d < 0 or d % SPACING or d // SPACING > k:
                continue
            s = d // SPACING
            if s > 0:
                both(c, s - 1, lambda cp: cp.wait_recv())
            if s == 1 and chunks[c][0] not in settled:
                settled.add(chunks[c][0])
                mine[chunks[c][0]].wait()
            if s < k:
                both(c, s, lambda cp: cp.start())
            else:
                arrived.append(c)
        run(tick, 2)
        stage_some(tick)
    tick = ticks
    while items:
        run(tick, 1)
        stage_some(tick)
        tick += 1
    for c in range(n):
        for s in range(k):
            both(c, s, lambda cp: cp.wait_send())
    settle(*list(pending))


def forward(cube, tokens, shards):
    width, hidden = tokens.shape[1], shards[5].shape[1]
    chunks = forward_chunks(width, hidden)
    n, k = len(chunks), cube.k
    cubed = (2,) * k
    act = lambda dtype: jax.ShapeDtypeStruct(tokens.shape, dtype)
    kinds = {"mid": act(F32)}
    kinds.update(dict.fromkeys(("g1", "g2", "prod"), jax.ShapeDtypeStruct((SEQ, hidden), BF16)))
    outs = [jax.ShapeDtypeStruct(cubed + s.shape, s.dtype) for s in shards]
    outs += [kinds.get(name, act(BF16)) for name in ACTS]
    got = pl.pallas_call(
        functools.partial(forward_kernel, cube, chunks),
        out_shape=tuple(outs),
        in_specs=[pl.BlockSpec(memory_space=pltpu.VMEM)] * 9,
        out_specs=tuple([pl.BlockSpec(memory_space=pl.ANY)] * len(outs)),
        scratch_shapes=[
            pltpu.VMEM(tokens.shape, BF16),
            pltpu.VMEM(tokens.shape, BF16),
            pltpu.VMEM(tokens.shape, BF16),
            pltpu.VMEM((SEQ, hidden), BF16),
            pltpu.VMEM((SEQ, hidden), BF16),
            pltpu.VMEM((SEQ, hidden), BF16),
            pltpu.VMEM(tokens.shape, F32),
            pltpu.VMEM(tokens.shape, F32),
            pltpu.VMEM(tokens.shape, F32),
            pltpu.VMEM((SLOTS,) + cubed + (shards[0].shape[0], width), BF16),
            pltpu.VMEM((SLOTS3,) + cubed + (shards[7].shape[0], 256), BF16),
            pltpu.SemaphoreType.DMA((n, k)),
            pltpu.SemaphoreType.DMA((n, k)),
            pltpu.SemaphoreType.DMA((8,)),
            pltpu.SemaphoreType.DMA((n + len(ACTS),)),
        ],
        compiler_params=pltpu.CompilerParams(
            collective_id=0, has_side_effects=True, vmem_limit_bytes=64 * 1024 * 1024 - 65536
        ),
        name="gather_and_forward",
    )(tokens, *shards)
    return got[:8], dict(zip(ACTS, got[8:]))


KEPT = ("nrm", "q", "sq", "k", "sk", "v", "sig", "att", "y", "mid", "n2", "g1", "g2", "prod")
PARTS, PARTS3, TILES, WIDE, WORK = 4, 2, 4, SEQ // SPAN, 2.0


def backward_chunks(width, hidden):
    chunks = [(7, c, 256) for c in range(0, width, 256)]
    pairs = [[(t, c, min(512, hidden - c)) for t in (5, 6)] for c in range(0, hidden, 512)]
    chunks[2:2] = pairs[0]
    for pair in pairs[1:]:
        chunks += pair
    chunks += [(t, c, 512) for t in (4, 3) for c in range(0, width, 512)]
    chunks += [(t, c, 512) for c in range(0, width, 512) for t in (0, 1, 2)]
    return chunks


class Tiles:
    def __init__(self, copies, ring, sources):
        self.copies, self.ring, self.sources = copies, ring, list(sources)
        self.slots, self.begun, self.used = ring.shape[0], [], 0
        self.fill()

    def fill(self):
        while len(self.begun) < min(len(self.sources), self.used + self.slots):
            i = len(self.begun)
            self.begun.append(self.copies.start(self.sources[i], self.ring.at[i % self.slots]))

    def take(self, act, count=1):
        given = range(self.used, self.used + count)
        for i in given:
            self.begun[i].wait()
        act(*(self.ring.at[i % self.slots] for i in given))
        self.used += count
        self.fill()


def backward_kernel(cube, chunks, *refs):
    cot, tok, weights = refs[0], refs[1], refs[2:10]
    acts = dict(zip(KEPT, refs[10 : 10 + len(KEPT)]))
    refs = refs[10 + len(KEPT) :]
    grad_tok, grads = refs[0], refs[1:9]
    a1, a2, a3, e0, e1, e2, nb, f1, f2, tiles, wide, slopes, sums, states = refs[9:23]
    part, part3, send, recv, local = refs[23:28]
    k, n = cube.k, len(chunks)
    landed = {False: refs[28 : 28 + k], True: refs[28 + k :]}
    cube.place()
    core = cube.bits[0]
    width, hidden = tok.shape[1], a1.shape[1]
    low, high = pl.ds(0, width), pl.ds(width, width)
    copies, loads = Copies(local), {}

    def load(name, dst, src=None):
        loads[name] = copies.start(acts[name] if src is None else src, dst)

    def need(*names):
        for name in names:
            if name in loads:
                loads.pop(name).wait()

    def rows_of(t, i):
        return weights[t].at[pl.ds(i * 256, 256), :]

    load("prod", a3)
    load("cot", e0, cot)
    blocks = width // 256
    order = [(7, i) for i in range(hidden // 256)] + [(4, i) for i in range(blocks)]
    order += [(t, i) for i in range(blocks) for t in range(4)]
    narrow = Tiles(copies, tiles, [rows_of(t, i) for t, i in order])
    load("g2", a2)
    load("g1", a1)
    load("n2", nb)
    broad = Tiles(copies, wide, [rows_of(t, i) for i in range(blocks) for t in (5, 6)])
    load("mid", f2)
    load("sig", e1)
    load("v", e2)
    heads = [acts[name].at[:, pl.ds(i * 256, 256)] for i in range(blocks) for name in ("sq", "sk")]
    slope = Tiles(copies, slopes, heads)
    cube.barrier()


    def tall(c):
        return chunks[c][0] == 7

    begins = [0] + [1 + 3 * s for s in range(k)]
    place = {}
    for c in range(n):
        place[c] = sum(tall(b) == tall(c) for b in range(c))

    def held(c, s, v, own):
        o = cube.kinds[c % 2][v][::-1]
        bit = cube.bits[o[s]] if own else 1 - cube.bits[o[s]]
        where = tuple(bit if b == o[s] else slice(None) for b in range(k - 1, -1, -1) if b not in o[:s])
        if s == 0:
            return (part3, (place[c] % PARTS3,) + where) if tall(c) else (part, (place[c] % PARTS,) + where)
        ref = landed[tall(c)][s - 1]
        return ref, (place[c] % ref.shape[0],) + where

    def arrival(c, s):
        ref = landed[tall(c)][s]
        return ref, (place[c] % ref.shape[0],) + (slice(None),) * (k - 1 - s)

    def copy(c, s, v):
        cols = (slice(None), pl.ds(0, chunks[c][2]))
        src, where = held(c, s, v, False)
        dst, there = arrival(c, s)
        return pltpu.make_async_remote_copy(
            src_ref=src.at[where + cols],
            dst_ref=dst.at[there + cols],
            send_sem=send.at[c, s],
            recv_sem=recv.at[c, s],
            device_id=cube.partner(cube.kinds[c % 2][v][::-1][s]),
            device_id_type=MESH,
        )

    def begin(c, s, v):
        copy(c, s, v).start()

    def finish(c, s, v):
        cp = copy(c, s, v)
        cp.wait_recv()
        cp.wait_send()
        t, c0, w = chunks[c]
        mine, where = held(c, s, v, True)
        into, there = arrival(c, s)

        def body(j, carry):
            cols = (slice(None), pl.ds(pl.multiple_of(j * 128, 128), 128))
            left, right = mine[where + cols], into[there + cols]
            if s == k - 1:
                to = pl.ds(pl.multiple_of(c0 + j * 128, 128), 128)
                grads[t][:, to] = left.astype(F32) + right.astype(F32)
            else:
                into[there + cols] = left + right
            return carry

        lax.fori_loop(0, w // 128, body, 0)

    def both(c, s, act):
        first, second = (o[::-1] for o in cube.kinds[c % 2])
        if first[s] == second[s] and set(first[:s]) == set(second[:s]):
            act(c, s, 0)
        else:

            @pl.when(core == 0)
            def _():
                act(c, s, 0)

            @pl.when(core == 1)
            def _():
                act(c, s, 1)


    def halves(count, body):
        def step(i, carry):
            body(i % 2, at_row(i % 2, 512))
            return carry

        lax.fori_loop(0, count * 2, step, 0)

    def rows(body):
        def step(i, carry):
            body(at_row(i, 128))
            return carry

        lax.fori_loop(0, SEQ // 128, step, 0)

    def product_grad(c):
        need("prod", "cot")
        _, c0, w = chunks[c]
        slot = place[c] % PARTS3

        def step(x, carry):
            left = a3[:, pl.ds(pl.multiple_of(x * (hidden // 2), 128), hidden // 2)]
            got = weight_grad(left, e0[:, pl.ds(c0, w)])
            got = got.reshape((2,) * (k - 1) + (-1, w)).astype(BF16)
            part3[(slot, x) + (slice(None),) * (k + 1)] = got
            return carry

        lax.fori_loop(0, 2, step, 0)

    def grad(c, names, left, lefts, right, rights=0):
        need(*names)
        _, c0, w = chunks[c]
        slot = place[c] % PARTS

        def step(i, carry):
            j, h = i // 2, i % 2
            at = pl.ds(pl.multiple_of(lefts + h * (width // 2), 128), width // 2)
            to = pl.ds(pl.multiple_of(rights + c0 + j * 256, 128), 256)
            got = weight_grad(left[:, at], right[..., to].reshape(-1, 256))
            got = got.reshape((2,) * (k - 1) + (-1, 256)).astype(BF16)
            dst = pl.ds(pl.multiple_of(j * 256, 128), 256)
            part[(slot, h) + (slice(None),) * k + (dst,)] = got
            return carry

        lax.fori_loop(0, w // 256 * 2, step, 0)

    def product_back(i):
        need("g1", "g2")
        to = pl.ds(i * 256, 256)

        def act(tile):
            def body(_, r):
                back = matmul_tr(e0[r, :], tile[...])
                one, two = a1[r, to].astype(F32), a2[r, to].astype(F32)
                a1[r, to] = (back * two).astype(BF16)
                a2[r, to] = (back * one).astype(BF16)

            halves(1, body)

        narrow.take(act)

    def hidden_back(i):
        to = pl.ds(i * 256, 256)

        def act(one, two):
            def body(_, r):
                f1[r, to] = (matmul_tr(a1[r, :], one[...]) + matmul_tr(a2[r, :], two[...])).astype(BF16)

            halves(1, body)

        broad.take(act, 2)

    def mid_back():
        need("mid")

        def body(r):
            mid = f2[r, :]
            back = e0[r, :].astype(F32) + scale_back(mid, row_scale(mid), f1[r, :].astype(F32))
            f1[r, :] = back.astype(BF16)
            e0[r, :] = back.astype(BF16)

        rows(body)

    def out_back(i):
        to = pl.ds(i * 256, 256)

        def act(tile):
            def body(_, r):
                f2[r, to] = matmul_tr(e0[r, :], tile[...])

            halves(1, body)

        narrow.take(act)

    def gate_back():
        need("att", "sig")

        def body(r):
            back, attn, sig = f2[r, :], a3[r, high].astype(F32), e1[r, :].astype(F32)
            scale = row_scale(attn)
            e1[r, :] = (back * (attn * scale) * sig * (1.0 - sig)).astype(BF16)
            a3[r, high] = scale_back(attn, scale, back * sig).astype(BF16)

        rows(body)

    def attend_back(i):
        need("q", "k", "v")
        mask, count = causal_pair(), SEQ // SPAN
        ats = [pl.ds(i * 256 + j * 128, 128) for j in range(2)]
        ups = [pl.ds(width + i * 256 + j * 128, 128) for j in range(2)]

        def act(sq, sk):
            def forth(b, carry):
                r = at_row(b, SPAN)
                got = [weight_grad(wide[b, :, up], e2[r, at]) for at, up in zip(ats, ups)]
                for j in range(2):
                    states[j, b] = sums[j].astype(BF16)
                    sums[j] += same_head(got[j])
                return carry

            def back(step, carry):
                b = count - 1 - step
                r = at_row(b, SPAN)
                new = []
                for j, (at, up) in enumerate(zip(ats, ups)):
                    q, kk, v, d = wide[b, :, at], wide[b, :, up], e2[r, at], a3[r, up]
                    keys, later, cols = two_heads(kk), sums[j], pl.ds(j * 128, 128)
                    d_kv = later.astype(BF16)
                    scores = jnp.where(mask, matmul_tr(q, keys), 0.0).astype(BF16)
                    d_scores = jnp.where(mask, matmul_tr(d, two_heads(v)), 0.0).astype(BF16)
                    dq = matmul(d_scores, keys) + matmul_tr(d, states[j, b])
                    dk = pick_heads(weight_grad(d_scores, q)) + matmul_tr(v, d_kv)
                    dv = pick_heads(weight_grad(scores, d)) + matmul(kk, d_kv)
                    dq = dq * sq[r, cols].astype(F32)
                    dk = dk * sk[r, cols].astype(F32)
                    new.append((dq, dk, dv, later + same_head(weight_grad(q, d))))
                for j, (at, up) in enumerate(zip(ats, ups)):
                    dq, dk, dv, later = new[j]
                    wide[b, :, at] = dq.astype(BF16)
                    wide[b, :, up] = dk.astype(BF16)
                    e2[r, at] = dv.astype(BF16)
                    sums[j] = later
                return carry

            sums[...] = jnp.zeros_like(sums)
            lax.fori_loop(0, count, forth, 0)
            sums[...] = jnp.zeros_like(sums)
            lax.fori_loop(0, count, back, 0)

        slope.take(act, 2)

    def normed_back(i):
        to = pl.ds(i * 256, 256)
        per = WIDE // 2
        lefts = (
            lambda h, r: wide[pl.ds(h * per, per), :, low].reshape(-1, width),
            lambda h, r: wide[pl.ds(h * per, per), :, high].reshape(-1, width),
            lambda h, r: e2[r, :],
            lambda h, r: e1[r, :],
        )
        for t, left in enumerate(lefts):

            def act(tile, t=t, left=left):
                def body(h, r):
                    got = matmul_tr(left(h, r), tile[...])
                    f2[r, to] = got if t == 0 else f2[r, to] + got

                halves(1, body)

            narrow.take(act)

    def token_back():
        need("tok")

        def body(r):
            x = e0[r, :].astype(F32)
            e0[r, :] = (f1[r, :].astype(F32) + scale_back(x, row_scale(x), f2[r, :])).astype(BF16)

        rows(body)
        load("end", grad_tok, e0)

    def after_product():
        load("y", a3.at[:, low])
        load("att", a3.at[:, high])

    def after_hidden():
        load("q", wide.at[:, :, low])
        load("k", wide.at[:, :, high])

    of = lambda *ts: [c for c in range(n) if chunks[c][0] in ts]
    last = blocks - 1
    items = [(("back", i), (), 0.9, functools.partial(product_back, i)) for i in range(hidden // 256)]
    items += [(("hidden", i), (), 3.0, functools.partial(hidden_back, i)) for i in range(blocks)]
    items.append(("mid", of(7), 2.5, mid_back))
    items += [(("out", i), (), 0.8, functools.partial(out_back, i)) for i in range(blocks)]
    items.append(("gate", ("product",), 2.5, gate_back))
    items += [(("attend", i), (), 5.0, functools.partial(attend_back, i)) for i in range(blocks)]
    items += [(("normed", i), (), 3.0, functools.partial(normed_back, i)) for i in range(blocks)]
    items.append(("tokens", ("tok",), 2.5, token_back))
    waiting = [
        ("product", of(7), after_product),
        ("heads", [("hidden", last)], after_hidden),
        ("nrm", of(5, 6), lambda: load("nrm", nb)),
        ("tok", of(4) + [("out", last)], lambda: load("tok", e0, tok)),
    ]

    def make(c):
        t, c0, w = chunks[c]
        if t == 7:
            return (), functools.partial(product_grad, c)
        if t in (5, 6):
            after = [("back", i) for i in range((c0 + w) // 256)]
            return after, functools.partial(grad, c, ("n2",), nb, 0, (a1, a2)[t - 5])
        if t == 4:
            return ("product", "mid"), functools.partial(grad, c, ("y",), a3, 0, e0)
        if t == 3:
            return ("gate", "nrm"), functools.partial(grad, c, ("nrm",), nb, 0, e1)
        after = ["nrm"] + [("attend", i) for i in range((c0 + w) // 256)]
        right, at = ((wide, 0), (wide, width), (e2, 0))[t]
        return after, functools.partial(grad, c, ("nrm",), nb, 0, right, at)

    done, made, first = set(), 0, {}
    tick = 0
    while items or made < n or any(tick <= first[c] + begins[k] for c in first):
        active = [(c, tick - first[c]) for c in sorted(first)]
        for c, d in active:
            if d in begins[1:]:
                both(c, begins.index(d) - 1, finish)
        for c, d in active:
            if d in begins[1:k]:
                both(c, begins.index(d), begin)
        if len(first) < made:
            c = len(first)
            first[c] = tick
            both(c, 0, begin)
        left = WORK

        def can_make():
            if made == n:
                return False
            busy = sum(
                tall(c) == tall(made) and not (c in first and tick >= first[c] + begins[1]) for c in range(made)
            )
            return busy < (PARTS3 if tall(made) else PARTS) and all(x in done for x in make(made)[0])

        while left > 0:
            if can_make() and made - len(first) < 2:
                make(made)[1]()
                done.add(made)
                made += 1
                left -= 2.0
            elif items and all(x in done for x in items[0][1]):
                name, _, cost, act = items.pop(0)
                act()
                done.add(name)
                left -= cost
            else:
                break
            for name, after, act in list(waiting):
                if all(x in done for x in after):
                    waiting.remove((name, after, act))
                    act()
                    done.add(name)
        tick += 1
    need(*list(loads))


def backward(cube, tokens, weights, acts, cotangent):
    width, hidden = tokens.shape[1], weights[5].shape[1]
    chunks = backward_chunks(width, hidden)
    n, k = len(chunks), cube.k
    devices = 1 << k
    few, many = width // devices, hidden // devices
    landed = []
    for slots, count, cols in (((5, 9, 10), few, 512), ((width // 256,), many, 256)):
        for s in range(k):
            shape = (slots[min(s, len(slots) - 1)],) + (2,) * (k - 1 - s) + (count, cols)
            landed.append(pltpu.VMEM(shape, BF16))
    shapes = [(few, width)] * 5 + [(few, hidden)] * 2 + [(many, width)]
    outs = [jax.ShapeDtypeStruct(tokens.shape, BF16)] + [jax.ShapeDtypeStruct(s, F32) for s in shapes]
    square, broad = pltpu.VMEM(tokens.shape, BF16), pltpu.VMEM((SEQ, hidden), BF16)
    local_copies = len(KEPT) + 1 + hidden // 256 + 9 * (width // 256)
    acts = {**acts, **{name: acts[name].reshape(WIDE, -1, width) for name in ("q", "k")}}
    return pl.pallas_call(
        functools.partial(backward_kernel, cube, chunks),
        out_shape=tuple(outs),
        in_specs=[pl.BlockSpec(memory_space=pl.ANY)] * (10 + len(KEPT)),
        out_specs=tuple(
            [pl.BlockSpec(memory_space=pl.ANY)] + [pl.BlockSpec(memory_space=pltpu.VMEM)] * 8
        ),
        scratch_shapes=[broad] * 3
        + [square] * 5
        + [pltpu.VMEM(tokens.shape, F32)]
        + [
            pltpu.VMEM((TILES, 256, width), BF16),
            pltpu.VMEM((WIDE, 256, hidden), BF16),
            pltpu.VMEM((4, SEQ, 256), BF16),
            pltpu.VMEM((2, 128, 128), F32),
            pltpu.VMEM((2, SEQ // SPAN, 128, 128), BF16),
            pltpu.VMEM((PARTS,) + (2,) * k + (few, 512), BF16),
            pltpu.VMEM((PARTS3,) + (2,) * k + (many, 256), BF16),
            pltpu.SemaphoreType.DMA((n, k)),
            pltpu.SemaphoreType.DMA((n, k)),
            pltpu.SemaphoreType.DMA((local_copies,)),
        ]
        + landed,
        compiler_params=pltpu.CompilerParams(
            collective_id=1, has_side_effects=True, vmem_limit_bytes=64 * 1024 * 1024 - 65536
        ),
        name="backward_and_sum",
    )(cotangent, tokens, *weights, *(acts[name] for name in KEPT))


def hand_over_kernel(count, *refs):
    held, sems = refs[2 * count : 3 * count], refs[3 * count]
    come = [pltpu.make_async_copy(refs[i], held[i], sems.at[0, i]) for i in range(count)]
    go = [pltpu.make_async_copy(held[i], refs[count + i], sems.at[1, i]) for i in range(count)]
    for copy in come:
        copy.start()
    for i in range(count):
        come[i].wait()
        go[i].start()
    for copy in go:
        copy.wait()


def hand_over(*arrays):
    count = len(arrays)
    return pl.pallas_call(
        functools.partial(hand_over_kernel, count),
        out_shape=tuple(jax.ShapeDtypeStruct(a.shape, a.dtype) for a in arrays),
        in_specs=[pl.BlockSpec(memory_space=pl.ANY)] * count,
        out_specs=tuple([pl.BlockSpec(memory_space=pl.ANY)] * count),
        scratch_shapes=[pltpu.VMEM(a.shape, a.dtype) for a in arrays]
        + [pltpu.SemaphoreType.DMA((2, count))],
        compiler_params=pltpu.CompilerParams(vmem_limit_bytes=64 * 1024 * 1024 - 65536),
        name="hand_over",
    )(*arrays)


def local(cube, tokens, w_query, w_key, w_value, w_gate, w_out, w_one, w_two, w_three, cotangent):
    shards = (w_query, w_key, w_value, w_gate, w_out, w_one, w_two, w_three)
    gathered, acts = forward(cube, tokens, shards)
    weights = [w.reshape(-1, w.shape[-1]) for w in gathered]
    return hand_over(acts["out"], *backward(cube, tokens, weights, acts, cotangent))


def solution(mesh):
    nd, nf = mesh.shape["dp"], mesh.shape["fsdp"]
    rows = P(("dp", "fsdp"), None)

    def step(*args):
        fits = args[1].shape[0] % 16 == 0 and args[8].shape[0] % 8 == 0 and args[0].shape[0] == SEQ
        if fits:
            return local(Cube(nd, nf), *args)
        return plain_local(*args)

    return jax.shard_map(
        step, mesh=mesh, in_specs=(rows,) * 10, out_specs=(rows,) * 10, check_vma=False
    )
```

```python
import functools

import jax
import jax.numpy as jnp
from jax import lax
from jax.experimental import pallas as pl
from jax.experimental.pallas import tpu as pltpu
from jax.sharding import PartitionSpec as P

HEADS = 16
HEAD = 64
BLOCK = 128
SEQ = 1024
SPAN = 256
EPS = 1e-06
MESH = pl.DeviceIdType.MESH
F32 = jnp.float32
BF16 = jnp.bfloat16


def row_scale(value):
    return lax.rsqrt(jnp.mean(value * value, axis=-1, keepdims=True) + EPS)


def scale_back(value, scale, grad):
    return scale * grad - value * scale * scale * scale * jnp.mean(
        grad * value, axis=-1, keepdims=True
    )


def logistic(value):
    return 1.0 / (1.0 + jnp.exp(-value))


def swish_slope(value):
    sig = logistic(value)
    return sig * (1.0 + value * (1.0 - sig))


def matmul(left, right):
    return jnp.dot(left, right, preferred_element_type=jnp.float32)


def matmul_tr(left, right):
    return lax.dot_general(
        left, right, (((1,), (1,)), ((), ())), preferred_element_type=jnp.float32
    )


def weight_grad(left, right):
    return lax.dot_general(
        left, right, (((0,), (0,)), ((), ())), preferred_element_type=jnp.float32
    )


class Cube:
    def __init__(self, nd, nf):
        self.nd, self.nf = nd, nf
        self.kd, self.kf = nd.bit_length() - 1, nf.bit_length() - 1
        self.k = self.kd + self.kf
        top = [self.kf - 1, self.kf - 2]
        outer = list(range(self.kf, self.k))
        mid = list(range(self.kf - 3, 0, -1))
        self.kinds = (
            (top + outer + mid + [0], top + mid + outer + [0]),
            (outer + top + mid + [0], mid + top + outer + [0]),
        )

    def place(self):
        self.x, self.f = lax.axis_index("dp"), lax.axis_index("fsdp")
        index = self.x * self.nf + self.f
        self.bits = [(index // (1 << b)) % 2 for b in range(self.k)]

    def partner(self, b):
        step = 1 - 2 * self.bits[b]
        if b < self.kf:
            return (self.x, self.f + step * (1 << b))
        return (self.x + step * (1 << (b - self.kf)), self.f)

    def at(self, free, flip=None):
        return tuple(
            slice(None) if b in free else (1 - self.bits[b] if b == flip else self.bits[b])
            for b in range(self.k - 1, -1, -1)
        )

    def barrier(self):
        sem = pltpu.get_barrier_semaphore()
        for b in range(self.k):
            pl.semaphore_signal(sem, inc=1, device_id=self.partner(b), device_id_type=MESH)
        pl.semaphore_wait(sem, self.k)


def at_row(i, size):
    return pl.ds(pl.multiple_of(i * size, size), size)


def head_masks(shape):
    lane = lax.broadcasted_iota(jnp.int32, shape, len(shape) - 1)
    return lane < HEAD


def two_heads(value):
    low = head_masks(value.shape)
    zero = jnp.zeros_like(value)
    return jnp.concatenate([jnp.where(low, value, zero), jnp.where(low, zero, value)], axis=0)


def pick_heads(value):
    rows = value.shape[0] // 2
    upper, lower = value[:rows], value[rows:]
    return jnp.where(head_masks(upper.shape), upper, lower)


def causal_pair():
    row = lax.broadcasted_iota(jnp.int32, (SPAN, 2 * SPAN), 0)
    col = lax.broadcasted_iota(jnp.int32, (SPAN, 2 * SPAN), 1)
    return row >= jnp.where(col >= SPAN, col - SPAN, col)


def same_head(value):
    row = lax.broadcasted_iota(jnp.int32, value.shape, 0)
    col = lax.broadcasted_iota(jnp.int32, value.shape, 1)
    return jnp.where((row < HEAD) == (col < HEAD), value, jnp.zeros_like(value))


def to_blocks(value):
    return value.reshape(-1, SEQ // BLOCK, BLOCK, HEADS, HEAD)


def plain_local(tokens, w_query, w_key, w_value, w_gate, w_out, w_one, w_two, w_three, cotangent):
    axes = ("dp", "fsdp")
    rows, width = w_query.shape
    hidden = w_one.shape[1]
    attn_all = lax.all_gather(
        jnp.concatenate((w_query, w_key, w_value, w_gate, w_out), axis=1), axes, axis=0, tiled=True
    )
    ffn_all = lax.all_gather(
        jnp.concatenate((w_one, w_two, w_three.reshape(rows, hidden)), axis=1),
        axes,
        axis=0,
        tiled=True,
    )
    wq, wk, wv, wu, wo = (attn_all[:, i * width : (i + 1) * width] for i in range(5))
    w1 = ffn_all[:, :hidden]
    w2 = ffn_all[:, hidden : 2 * hidden]
    w3 = ffn_all[:, 2 * hidden :].reshape(hidden, width)
    x = tokens.astype(jnp.float32)
    scale_one = row_scale(x)
    normed = (x * scale_one).astype(jnp.bfloat16)
    pre_q = matmul(normed, wq)
    pre_k = matmul(normed, wk)
    pre_v = matmul(normed, wv)
    pre_u = matmul(normed, wu)
    q_blocks = to_blocks((pre_q * logistic(pre_q)).astype(jnp.bfloat16))
    k_blocks = to_blocks((pre_k * logistic(pre_k)).astype(jnp.bfloat16))
    v_blocks = to_blocks(pre_v.astype(jnp.bfloat16))
    causal = jnp.tril(jnp.ones((BLOCK, BLOCK), jnp.float32))
    scores = (
        jnp.einsum("bnchd,bnehd->bnhce", q_blocks, k_blocks, preferred_element_type=jnp.float32)
        * causal
    ).astype(jnp.bfloat16)
    inner = jnp.einsum("bnhce,bnehd->bnchd", scores, v_blocks, preferred_element_type=jnp.float32)
    block_kv = jnp.einsum(
        "bnchd,bnche->bnhde", k_blocks, v_blocks, preferred_element_type=jnp.float32
    )
    state = (jnp.cumsum(block_kv, axis=1) - block_kv).astype(jnp.bfloat16)
    outer = jnp.einsum("bnchd,bnhde->bnche", q_blocks, state, preferred_element_type=jnp.float32)
    attn = (inner + outer).reshape(x.shape)
    scale_two = row_scale(attn)
    attn_normed = attn * scale_two
    sig = logistic(pre_u)
    gated = (attn_normed * sig).astype(jnp.bfloat16)
    mid = x + matmul(gated, wo)
    scale_three = row_scale(mid)
    normed_two = (mid * scale_three).astype(jnp.bfloat16)
    first = matmul(normed_two, w1)
    second = matmul(normed_two, w2)
    product = (first * second).astype(jnp.bfloat16)
    output = (mid + matmul(product, w3)).astype(jnp.bfloat16)
    grad_three = weight_grad(product, cotangent)
    dprod = matmul_tr(cotangent, w3)
    d_first = (dprod * second).astype(jnp.bfloat16)
    d_second = (dprod * first).astype(jnp.bfloat16)
    grad_one = weight_grad(normed_two, d_first)
    grad_two = weight_grad(normed_two, d_second)
    d_normed_two = matmul_tr(d_first, w1) + matmul_tr(d_second, w2)
    d_mid = cotangent.astype(jnp.float32) + scale_back(mid, scale_three, d_normed_two)
    d_branch = d_mid.astype(jnp.bfloat16)
    grad_out = weight_grad(gated, d_branch)
    d_gated = matmul_tr(d_branch, wo)
    d_pre_u = (d_gated * attn_normed * sig * (1.0 - sig)).astype(jnp.bfloat16)
    d_attn = scale_back(attn, scale_two, d_gated * sig).astype(jnp.bfloat16)
    d_blocks = to_blocks(d_attn)
    d_scores = (
        jnp.einsum("bnchd,bnehd->bnhce", d_blocks, v_blocks, preferred_element_type=jnp.float32)
        * causal
    ).astype(jnp.bfloat16)
    d_state = jnp.einsum(
        "bnchd,bnche->bnhde", q_blocks, d_blocks, preferred_element_type=jnp.float32
    )
    d_kv = (lax.cumsum(d_state, axis=1, reverse=True) - d_state).astype(jnp.bfloat16)
    dq_full = jnp.einsum(
        "bnhce,bnehd->bnchd", d_scores, k_blocks, preferred_element_type=jnp.float32
    ) + jnp.einsum("bnche,bnhde->bnchd", d_blocks, state, preferred_element_type=jnp.float32)
    dk_full = jnp.einsum(
        "bnhce,bnchd->bnehd", d_scores, q_blocks, preferred_element_type=jnp.float32
    ) + jnp.einsum("bnche,bnhde->bnchd", v_blocks, d_kv, preferred_element_type=jnp.float32)
    dv_full = jnp.einsum(
        "bnhce,bnchd->bnehd", scores, d_blocks, preferred_element_type=jnp.float32
    ) + jnp.einsum("bnchd,bnhde->bnche", k_blocks, d_kv, preferred_element_type=jnp.float32)
    d_query = (dq_full.reshape(x.shape) * swish_slope(pre_q)).astype(jnp.bfloat16)
    d_key = (dk_full.reshape(x.shape) * swish_slope(pre_k)).astype(jnp.bfloat16)
    d_value = dv_full.reshape(x.shape).astype(jnp.bfloat16)
    grad_query = weight_grad(normed, d_query)
    grad_key = weight_grad(normed, d_key)
    grad_value = weight_grad(normed, d_value)
    grad_gate = weight_grad(normed, d_pre_u)
    d_normed = (
        matmul_tr(d_query, wq)
        + matmul_tr(d_key, wk)
        + matmul_tr(d_value, wv)
        + matmul_tr(d_pre_u, wu)
    )
    grad_tokens = (d_mid + scale_back(x, scale_one, d_normed)).astype(jnp.bfloat16)
    half = jnp.bfloat16
    ffn_grads = jnp.concatenate(
        (
            grad_one.astype(half),
            grad_two.astype(half),
            grad_three.astype(half).reshape(width, hidden),
        ),
        axis=1,
    )
    attn_grads = jnp.concatenate(
        [g.astype(half) for g in (grad_query, grad_key, grad_value, grad_gate, grad_out)], axis=1
    )
    ffn_sum = lax.psum_scatter(ffn_grads, axes, scatter_dimension=0, tiled=True)
    attn_sum = lax.psum_scatter(attn_grads, axes, scatter_dimension=0, tiled=True)
    ffn_sum = ffn_sum.astype(jnp.float32)
    attn_sum = attn_sum.astype(jnp.float32)
    shares = tuple(attn_sum[:, i * width : (i + 1) * width] for i in range(5)) + (
        ffn_sum[:, :hidden],
        ffn_sum[:, hidden : 2 * hidden],
        ffn_sum[:, 2 * hidden :].reshape(w_three.shape),
    )
    return (
        output,
        grad_tokens,
        shares[0],
        shares[1],
        shares[2],
        shares[3],
        shares[4],
        shares[5],
        shares[6],
        shares[7],
    )


class Copies:
    def __init__(self, sems):
        self.sems, self.count = sems, 0

    def start(self, src, dst):
        copy = pltpu.make_async_copy(src, dst, self.sems.at[self.count])
        self.count += 1
        copy.start()
        return copy


def forward_chunks(width, hidden):
    chunks = []
    for t in range(5):
        chunks += [(t, c, width // 2) for c in range(0, width, width // 2)]
    for c in range(0, hidden, width):
        size = min(width, hidden - c)
        chunks += [(5, c, size), (6, c, size)]
    chunks += [(7, c, 256) for c in range(0, width, 256)]
    return chunks


SLOTS, SLOTS3, SPACING = 5, 3, 2
ACTS = ("nrm", "q", "sq", "k", "sk", "v", "sig", "att", "y", "mid", "n2", "g1", "g2", "prod", "out")


def forward_kernel(cube, chunks, *refs):
    tok, shards = refs[0], refs[1:9]
    weights = refs[9:17]
    acts = dict(zip(ACTS, refs[17 : 17 + len(ACTS)]))
    (nb, ab, sb, a1, a2, a3, fu, fa, fm, stage, stage3, send, recv, own, local) = refs[17 + len(ACTS) :]
    cube.place()
    core, k, n = cube.bits[0], cube.k, len(chunks)
    width = tok.shape[1]
    mine = []
    for t in range(8):
        mine.append(pltpu.make_async_copy(shards[t], weights[t].at[cube.at(())], own.at[t]))
        mine[-1].start()
    cube.barrier()
    copies = Copies(local)


    def copy(c, s, v):
        t, c0, w = chunks[c]
        order = cube.kinds[c % 2][v]
        where = cube.at(order[:s]) + (slice(None), pl.ds(c0, w))
        src = shards[t].at[:, pl.ds(c0, w)] if s == 0 else weights[t].at[where]
        return pltpu.make_async_remote_copy(
            src_ref=src,
            dst_ref=weights[t].at[where],
            send_sem=send.at[c, s],
            recv_sem=recv.at[c, s],
            device_id=cube.partner(order[s]),
            device_id_type=MESH,
        )

    def both(c, s, act):
        first, second = cube.kinds[c % 2]
        if first[s] == second[s] and set(first[:s]) == set(second[:s]):
            act(copy(c, s, 0))
        else:

            @pl.when(core == 0)
            def _():
                act(copy(c, s, 0))

            @pl.when(core == 1)
            def _():
                act(copy(c, s, 1))


    whole = (slice(None),) * (k + 1)
    pending = {}

    def out_of(name, src):
        pending[name] = copies.start(src, acts[name])

    def settle(*names):
        for name in names:
            if name in pending:
                pending.pop(name).wait()

    def cols(ref, c, w):
        return ref[whole + (pl.ds(pl.multiple_of(c, 256), w),)].reshape(-1, w)

    def tiles(total, body):
        def step(i, carry):
            body(i // 2, i % 2)
            return carry

        lax.fori_loop(0, total // 256 * 2, step, 0)

    def rows(body, size=128):
        def step(i, carry):
            body(at_row(i, size))
            return carry

        lax.fori_loop(0, SEQ // size, step, 0)

    def norm_one():
        def body(r):
            x = tok[r, :].astype(F32)
            nb[r, :] = (x * row_scale(x)).astype(BF16)

        rows(body)
        out_of("nrm", nb)

    def project(t, c0, w, ref):
        def body(j, h):
            r = at_row(h, 512)
            to = pl.ds(pl.multiple_of(c0 + j * 256, 256), 256)
            acc = matmul(nb[r, :], cols(ref, j * 256, 256))
            if t == 3:
                fu[r, to] = acc
            elif t == 2:
                a3[r, to] = acc.astype(BF16)
            else:
                slope_to = pl.ds(pl.multiple_of(width + c0 + j * 256, 256), 256)
                sig = logistic(acc)
                dst = a1 if t == 0 else a2
                dst[r, to] = (acc * sig).astype(BF16)
                dst[r, slope_to] = (sig * (1.0 + acc * (1.0 - sig))).astype(BF16)

        tiles(w, body)
        if c0 + w == width:
            if t == 2:
                out_of("v", a3.at[:, pl.ds(0, width)])
            elif t < 2:
                src = a1 if t == 0 else a2
                out_of("qk"[t], src.at[:, pl.ds(0, width)])
                out_of(("sq", "sk")[t], src.at[:, pl.ds(width, width)])

    def attend(first, last):
        mask = causal_pair()

        def pair(p, carry):
            at = pl.ds(pl.multiple_of(p * 128, 128), 128)
            state = jnp.zeros((128, 128), F32)
            for b in range(SEQ // SPAN):
                r = pl.ds(b * SPAN, SPAN)
                q, kk, v = a1[r, at], a2[r, at], a3[r, at]
                scores = jnp.where(mask, matmul_tr(q, two_heads(kk)), 0.0).astype(BF16)
                acc = matmul(scores, two_heads(v))
                if b > 0:
                    acc += matmul(q, state.astype(BF16))
                fa[r, at] = acc
                if b + 1 < SEQ // SPAN:
                    state += same_head(weight_grad(kk, v))
            return carry

        lax.fori_loop(first, last, pair, 0)
    def gate():
        def body(r):
            attn, sig = fa[r, :], logistic(fu[r, :])
            a3[r, pl.ds(width, width)] = (attn * row_scale(attn) * sig).astype(BF16)
            ab[r, :] = attn.astype(BF16)
            sb[r, :] = sig.astype(BF16)

        rows(body)
        out_of("att", ab)
        out_of("sig", sb)
        out_of("y", a3.at[:, pl.ds(width, width)])

    def project_out(c0, w, ref):
        def body(j, h):
            r = at_row(h, 512)
            to = pl.ds(pl.multiple_of(c0 + j * 256, 256), 256)
            fm[r, to] = tok[r, to].astype(F32) + matmul(
                a3[r, pl.ds(width, width)], cols(ref, j * 256, 256)
            )

        tiles(w, body)

    def norm_two():
        settle("nrm")

        def body(r):
            mid = fm[r, :]
            nb[r, :] = (mid * row_scale(mid)).astype(BF16)

        rows(body)
        out_of("mid", fm)
        out_of("n2", nb)
        settle("q", "sq", "k", "sk", "v", "y")

    def hidden(c0, w, one, two):
        def body(j, h):
            r = at_row(h, 512)
            to = pl.ds(pl.multiple_of(c0 + j * 256, 256), 256)
            first = matmul(nb[r, :], cols(one, j * 256, 256))
            second = matmul(nb[r, :], cols(two, j * 256, 256))
            a1[r, to] = first.astype(BF16)
            a2[r, to] = second.astype(BF16)
            a3[r, to] = (first * second).astype(BF16)

        tiles(w, body)
        if c0 + w == a1.shape[1]:
            out_of("g1", a1)
            out_of("g2", a2)
            out_of("prod", a3)
            settle("n2")

    def down(c0, w, ref):
        def body(j, h):
            r = at_row(h, 512)
            to = pl.ds(pl.multiple_of(c0 + j * 256, 256), 256)
            nb[r, to] = (fm[r, to] + matmul(a3[r, :], cols(ref, j * 256, 256))).astype(BF16)

        tiles(w, body)
        if c0 + w == width:
            out_of("out", nb)

    index = {(t, c0): i for i, (t, c0, w) in enumerate(chunks)}
    items = [((), norm_one)]
    for i, (t, c0, w) in enumerate(chunks):
        last = c0 + w == width
        if t < 4:
            items.append(((i,), functools.partial(project, t, c0, w)))
            if t == 2 and last:
                items += [((), functools.partial(attend, 0, 4)), ((), functools.partial(attend, 4, 8))]
            if t == 3 and last:
                items.append(((), gate))
        elif t == 4:
            items.append(((i,), functools.partial(project_out, c0, w)))
            if last:
                items.append(((), norm_two))
        elif t == 5:
            items.append(((i, index[6, c0]), functools.partial(hidden, c0, w)))
        elif t == 7:
            items.append(((i,), functools.partial(down, c0, w)))

    free = {False: list(range(SLOTS)), True: list(range(SLOTS3))}
    arrived, staged = [], {}

    def stage_some(tick):
        while arrived and free[chunks[arrived[0]][0] == 7]:
            c = arrived.pop(0)
            t, c0, w = chunks[c]
            slot = free[t == 7].pop(0)
            dst = (stage3 if t == 7 else stage).at[(slot,) + whole + (pl.ds(0, w),)]
            cp = copies.start(weights[t].at[whole + (pl.ds(c0, w),)], dst)
            staged[c] = (tick, slot, cp)

    def run(tick, budget):
        while items and budget > 0:
            needs, act = items[0]
            if any(c not in staged or staged[c][0] >= tick for c in needs):
                return
            items.pop(0)
            given = []
            for c in needs:
                _, slot, cp = staged[c]
                cp.wait()
                given.append((stage3 if chunks[c][0] == 7 else stage).at[slot])
            act(*given)
            for c in needs:
                free[chunks[c][0] == 7].append(staged[c][1])
            budget -= 1

    settled = set()
    steps = [SPACING * s for s in range(k)]
    steps.append(steps[-1] + 1)
    ticks = n + steps[-1]
    for tick in range(ticks):
        for c in range(n):
            d = tick - c
            if d not in steps:
                continue
            s = steps.index(d)
            if s > 0:
                both(c, s - 1, lambda cp: cp.wait_recv())
            if s == 1 and chunks[c][0] not in settled:
                settled.add(chunks[c][0])
                mine[chunks[c][0]].wait()
            if s < k:
                both(c, s, lambda cp: cp.start())
            else:
                arrived.append(c)
        run(tick, 2)
        stage_some(tick)
    tick = ticks
    while items:
        run(tick, 1)
        stage_some(tick)
        tick += 1
    for c in range(n):
        for s in range(k):
            both(c, s, lambda cp: cp.wait_send())
    settle(*list(pending))


def forward(cube, tokens, shards):
    width, hidden = tokens.shape[1], shards[5].shape[1]
    chunks = forward_chunks(width, hidden)
    n, k = len(chunks), cube.k
    cubed = (2,) * k
    act = lambda dtype: jax.ShapeDtypeStruct(tokens.shape, dtype)
    kinds = {"mid": act(F32)}
    kinds.update(dict.fromkeys(("g1", "g2", "prod"), jax.ShapeDtypeStruct((SEQ, hidden), BF16)))
    outs = [jax.ShapeDtypeStruct(cubed + s.shape, s.dtype) for s in shards]
    outs += [kinds.get(name, act(BF16)) for name in ACTS]
    got = pl.pallas_call(
        functools.partial(forward_kernel, cube, chunks),
        out_shape=tuple(outs),
        in_specs=[pl.BlockSpec(memory_space=pltpu.VMEM)] * 9,
        out_specs=tuple([pl.BlockSpec(memory_space=pl.ANY)] * len(outs)),
        scratch_shapes=[
            pltpu.VMEM(tokens.shape, BF16),
            pltpu.VMEM(tokens.shape, BF16),
            pltpu.VMEM(tokens.shape, BF16),
            pltpu.VMEM((SEQ, hidden), BF16),
            pltpu.VMEM((SEQ, hidden), BF16),
            pltpu.VMEM((SEQ, hidden), BF16),
            pltpu.VMEM(tokens.shape, F32),
            pltpu.VMEM(tokens.shape, F32),
            pltpu.VMEM(tokens.shape, F32),
            pltpu.VMEM((SLOTS,) + cubed + (shards[0].shape[0], width), BF16),
            pltpu.VMEM((SLOTS3,) + cubed + (shards[7].shape[0], 256), BF16),
            pltpu.SemaphoreType.DMA((n, k)),
            pltpu.SemaphoreType.DMA((n, k)),
            pltpu.SemaphoreType.DMA((8,)),
            pltpu.SemaphoreType.DMA((n + len(ACTS),)),
        ],
        compiler_params=pltpu.CompilerParams(
            collective_id=0, has_side_effects=True, vmem_limit_bytes=64 * 1024 * 1024 - 65536
        ),
        name="gather_and_forward",
    )(tokens, *shards)
    return got[:8], dict(zip(ACTS, got[8:]))


KEPT = ("nrm", "q", "sq", "k", "sk", "v", "sig", "att", "y", "mid", "n2", "g1", "g2", "prod")
PARTS, PARTS3, TILES, WIDE, WORK = 4, 2, 4, SEQ // SPAN, 2.5


def backward_chunks(width, hidden):
    chunks = [(7, c, 256) for c in range(0, width, 256)]
    pairs = [[(t, c, min(512, hidden - c)) for t in (5, 6)] for c in range(0, hidden, 512)]
    chunks[2:2] = pairs[0]
    for pair in pairs[1:]:
        chunks += pair
    chunks += [(t, c, 512) for t in (4, 3) for c in range(0, width, 512)]
    chunks += [(t, c, 512) for c in range(0, width, 512) for t in (0, 1, 2)]
    return chunks


class Tiles:
    def __init__(self, copies, ring, sources):
        self.copies, self.ring, self.sources = copies, ring, list(sources)
        self.slots, self.begun, self.used = ring.shape[0], [], 0
        self.fill()

    def fill(self):
        while len(self.begun) < min(len(self.sources), self.used + self.slots):
            i = len(self.begun)
            self.begun.append(self.copies.start(self.sources[i], self.ring.at[i % self.slots]))

    def take(self, act, count=1):
        given = range(self.used, self.used + count)
        for i in given:
            self.begun[i].wait()
        act(*(self.ring.at[i % self.slots] for i in given))
        self.used += count
        self.fill()


def backward_kernel(cube, chunks, *refs):
    cot, tok, weights = refs[0], refs[1], refs[2:10]
    acts = dict(zip(KEPT, refs[10 : 10 + len(KEPT)]))
    refs = refs[10 + len(KEPT) :]
    grad_tok, grads = refs[0], refs[1:9]
    a1, a2, a3, e0, e1, e2, nb, f1, f2, tiles, wide, slopes, sums, states = refs[9:23]
    part, part3, send, recv, local = refs[23:28]
    k, n = cube.k, len(chunks)
    landed = {False: refs[28 : 28 + k], True: refs[28 + k :]}
    cube.place()
    core = cube.bits[0]
    width, hidden = tok.shape[1], a1.shape[1]
    low, high = pl.ds(0, width), pl.ds(width, width)
    copies, loads = Copies(local), {}

    def load(name, dst, src=None):
        loads[name] = copies.start(acts[name] if src is None else src, dst)

    def need(*names):
        for name in names:
            if name in loads:
                loads.pop(name).wait()

    def rows_of(t, i):
        return weights[t].at[pl.ds(i * 256, 256), :]

    load("prod", a3)
    load("cot", e0, cot)
    blocks = width // 256
    order = [(7, i) for i in range(hidden // 256)] + [(4, i) for i in range(blocks)]
    order += [(t, i) for i in range(blocks) for t in range(4)]
    narrow = Tiles(copies, tiles, [rows_of(t, i) for t, i in order])
    load("g2", a2)
    load("g1", a1)
    load("n2", nb)
    broad = Tiles(copies, wide, [rows_of(t, i) for i in range(blocks) for t in (5, 6)])
    load("mid", f2)
    load("sig", e1)
    load("v", e2)
    heads = [acts[name].at[:, pl.ds(i * 256, 256)] for i in range(blocks) for name in ("sq", "sk")]
    slope = Tiles(copies, slopes, heads)
    cube.barrier()


    def tall(c):
        return chunks[c][0] == 7

    begins = [0] + [1 + 3 * s for s in range(k)]
    place = {}
    for c in range(n):
        place[c] = sum(tall(b) == tall(c) for b in range(c))

    def held(c, s, v, own):
        o = cube.kinds[c % 2][v][::-1]
        bit = cube.bits[o[s]] if own else 1 - cube.bits[o[s]]
        where = tuple(bit if b == o[s] else slice(None) for b in range(k - 1, -1, -1) if b not in o[:s])
        if s == 0:
            return (part3, (place[c] % PARTS3,) + where) if tall(c) else (part, (place[c] % PARTS,) + where)
        ref = landed[tall(c)][s - 1]
        return ref, (place[c] % ref.shape[0],) + where

    def arrival(c, s):
        ref = landed[tall(c)][s]
        return ref, (place[c] % ref.shape[0],) + (slice(None),) * (k - 1 - s)

    def copy(c, s, v):
        cols = (slice(None), pl.ds(0, chunks[c][2]))
        src, where = held(c, s, v, False)
        dst, there = arrival(c, s)
        return pltpu.make_async_remote_copy(
            src_ref=src.at[where + cols],
            dst_ref=dst.at[there + cols],
            send_sem=send.at[c, s],
            recv_sem=recv.at[c, s],
            device_id=cube.partner(cube.kinds[c % 2][v][::-1][s]),
            device_id_type=MESH,
        )

    def begin(c, s, v):
        copy(c, s, v).start()

    def finish(c, s, v):
        cp = copy(c, s, v)
        cp.wait_recv()
        cp.wait_send()
        t, c0, w = chunks[c]
        mine, where = held(c, s, v, True)
        into, there = arrival(c, s)

        def body(j, carry):
            cols = (slice(None), pl.ds(pl.multiple_of(j * 128, 128), 128))
            left, right = mine[where + cols], into[there + cols]
            if s == k - 1:
                to = pl.ds(pl.multiple_of(c0 + j * 128, 128), 128)
                grads[t][:, to] = left.astype(F32) + right.astype(F32)
            else:
                into[there + cols] = left + right
            return carry

        lax.fori_loop(0, w // 128, body, 0)

    def both(c, s, act):
        first, second = (o[::-1] for o in cube.kinds[c % 2])
        if first[s] == second[s] and set(first[:s]) == set(second[:s]):
            act(c, s, 0)
        else:

            @pl.when(core == 0)
            def _():
                act(c, s, 0)

            @pl.when(core == 1)
            def _():
                act(c, s, 1)


    def halves(count, body):
        def step(i, carry):
            body(i % 2, at_row(i % 2, 512))
            return carry

        lax.fori_loop(0, count * 2, step, 0)

    def rows(body):
        def step(i, carry):
            body(at_row(i, 128))
            return carry

        lax.fori_loop(0, SEQ // 128, step, 0)

    def product_grad(c):
        need("prod", "cot")
        _, c0, w = chunks[c]
        slot = place[c] % PARTS3

        def step(x, carry):
            left = a3[:, pl.ds(pl.multiple_of(x * (hidden // 2), 128), hidden // 2)]
            got = weight_grad(left, e0[:, pl.ds(c0, w)])
            got = got.reshape((2,) * (k - 1) + (-1, w)).astype(BF16)
            part3[(slot, x) + (slice(None),) * (k + 1)] = got
            return carry

        lax.fori_loop(0, 2, step, 0)

    def grad(c, names, left, lefts, right, rights=0):
        need(*names)
        _, c0, w = chunks[c]
        slot = place[c] % PARTS

        def step(i, carry):
            j, h = i // 2, i % 2
            at = pl.ds(pl.multiple_of(lefts + h * (width // 2), 128), width // 2)
            to = pl.ds(pl.multiple_of(rights + c0 + j * 256, 128), 256)
            got = weight_grad(left[:, at], right[..., to].reshape(-1, 256))
            got = got.reshape((2,) * (k - 1) + (-1, 256)).astype(BF16)
            dst = pl.ds(pl.multiple_of(j * 256, 128), 256)
            part[(slot, h) + (slice(None),) * k + (dst,)] = got
            return carry

        lax.fori_loop(0, w // 256 * 2, step, 0)

    def product_back(i):
        need("g1", "g2")
        to = pl.ds(i * 256, 256)

        def act(tile):
            def body(_, r):
                back = matmul_tr(e0[r, :], tile[...])
                one, two = a1[r, to].astype(F32), a2[r, to].astype(F32)
                a1[r, to] = (back * two).astype(BF16)
                a2[r, to] = (back * one).astype(BF16)

            halves(1, body)

        narrow.take(act)

    def hidden_back(i):
        to = pl.ds(i * 256, 256)

        def act(one, two):
            def body(_, r):
                f1[r, to] = (matmul_tr(a1[r, :], one[...]) + matmul_tr(a2[r, :], two[...])).astype(BF16)

            halves(1, body)

        broad.take(act, 2)

    def mid_back():
        need("mid")

        def body(r):
            mid = f2[r, :]
            back = e0[r, :].astype(F32) + scale_back(mid, row_scale(mid), f1[r, :].astype(F32))
            f1[r, :] = back.astype(BF16)
            e0[r, :] = back.astype(BF16)

        rows(body)

    def out_back(i):
        to = pl.ds(i * 256, 256)

        def act(tile):
            def body(_, r):
                f2[r, to] = matmul_tr(e0[r, :], tile[...])

            halves(1, body)

        narrow.take(act)

    def gate_back():
        need("att", "sig")

        def body(r):
            back, attn, sig = f2[r, :], a3[r, high].astype(F32), e1[r, :].astype(F32)
            scale = row_scale(attn)
            e1[r, :] = (back * (attn * scale) * sig * (1.0 - sig)).astype(BF16)
            a3[r, high] = scale_back(attn, scale, back * sig).astype(BF16)

        rows(body)

    def attend_back(i):
        need("q", "k", "v")
        mask, count = causal_pair(), SEQ // SPAN
        ats = [pl.ds(i * 256 + j * 128, 128) for j in range(2)]
        ups = [pl.ds(width + i * 256 + j * 128, 128) for j in range(2)]

        def act(sq, sk):
            def forth(b, carry):
                r = at_row(b, SPAN)
                got = [weight_grad(wide[b, :, up], e2[r, at]) for at, up in zip(ats, ups)]
                for j in range(2):
                    states[j, b] = sums[j].astype(BF16)
                    sums[j] += same_head(got[j])
                return carry

            def back(step, carry):
                b = count - 1 - step
                r = at_row(b, SPAN)
                new = []
                for j, (at, up) in enumerate(zip(ats, ups)):
                    q, kk, v, d = wide[b, :, at], wide[b, :, up], e2[r, at], a3[r, up]
                    keys, later, cols = two_heads(kk), sums[j], pl.ds(j * 128, 128)
                    d_kv = later.astype(BF16)
                    scores = jnp.where(mask, matmul_tr(q, keys), 0.0).astype(BF16)
                    d_scores = jnp.where(mask, matmul_tr(d, two_heads(v)), 0.0).astype(BF16)
                    dq = matmul(d_scores, keys) + matmul_tr(d, states[j, b])
                    dk = pick_heads(weight_grad(d_scores, q)) + matmul_tr(v, d_kv)
                    dv = pick_heads(weight_grad(scores, d)) + matmul(kk, d_kv)
                    dq = dq * sq[r, cols].astype(F32)
                    dk = dk * sk[r, cols].astype(F32)
                    new.append((dq, dk, dv, later + same_head(weight_grad(q, d))))
                for j, (at, up) in enumerate(zip(ats, ups)):
                    dq, dk, dv, later = new[j]
                    wide[b, :, at] = dq.astype(BF16)
                    wide[b, :, up] = dk.astype(BF16)
                    e2[r, at] = dv.astype(BF16)
                    sums[j] = later
                return carry

            sums[...] = jnp.zeros_like(sums)
            lax.fori_loop(0, count, forth, 0)
            sums[...] = jnp.zeros_like(sums)
            lax.fori_loop(0, count, back, 0)

        slope.take(act, 2)

    def normed_back(i):
        to = pl.ds(i * 256, 256)
        per = WIDE // 2
        lefts = (
            lambda h, r: wide[pl.ds(h * per, per), :, low].reshape(-1, width),
            lambda h, r: wide[pl.ds(h * per, per), :, high].reshape(-1, width),
            lambda h, r: e2[r, :],
            lambda h, r: e1[r, :],
        )
        for t, left in enumerate(lefts):

            def act(tile, t=t, left=left):
                def body(h, r):
                    got = matmul_tr(left(h, r), tile[...])
                    f2[r, to] = got if t == 0 else f2[r, to] + got

                halves(1, body)

            narrow.take(act)

    def token_back():
        need("tok")

        def body(r):
            x = e0[r, :].astype(F32)
            e0[r, :] = (f1[r, :].astype(F32) + scale_back(x, row_scale(x), f2[r, :])).astype(BF16)

        rows(body)
        load("end", grad_tok, e0)

    def after_product():
        load("y", a3.at[:, low])
        load("att", a3.at[:, high])

    def after_hidden():
        load("q", wide.at[:, :, low])
        load("k", wide.at[:, :, high])

    of = lambda *ts: [c for c in range(n) if chunks[c][0] in ts]
    last = blocks - 1
    items = [(("back", i), (), 0.9, functools.partial(product_back, i)) for i in range(hidden // 256)]
    items += [(("hidden", i), (), 3.0, functools.partial(hidden_back, i)) for i in range(blocks)]
    items.append(("mid", of(7), 2.5, mid_back))
    items += [(("out", i), (), 0.8, functools.partial(out_back, i)) for i in range(blocks)]
    items.append(("gate", ("product",), 2.5, gate_back))
    items += [(("attend", i), (), 5.0, functools.partial(attend_back, i)) for i in range(blocks)]
    items += [(("normed", i), (), 3.0, functools.partial(normed_back, i)) for i in range(blocks)]
    items.append(("tokens", ("tok",), 2.5, token_back))
    waiting = [
        ("product", of(7), after_product),
        ("heads", [("hidden", last)], after_hidden),
        ("nrm", of(5, 6), lambda: load("nrm", nb)),
        ("tok", of(4) + [("out", last)], lambda: load("tok", e0, tok)),
    ]

    def make(c):
        t, c0, w = chunks[c]
        if t == 7:
            return (), functools.partial(product_grad, c)
        if t in (5, 6):
            after = [("back", i) for i in range((c0 + w) // 256)]
            return after, functools.partial(grad, c, ("n2",), nb, 0, (a1, a2)[t - 5])
        if t == 4:
            return ("product", "mid"), functools.partial(grad, c, ("y",), a3, 0, e0)
        if t == 3:
            return ("gate", "nrm"), functools.partial(grad, c, ("nrm",), nb, 0, e1)
        after = ["nrm"] + [("attend", i) for i in range((c0 + w) // 256)]
        right, at = ((wide, 0), (wide, width), (e2, 0))[t]
        return after, functools.partial(grad, c, ("nrm",), nb, 0, right, at)

    done, made, first = set(), 0, {}
    tick = 0
    while items or made < n or any(tick <= first[c] + begins[k] for c in first):
        active = [(c, tick - first[c]) for c in sorted(first)]
        for c, d in active:
            if d in begins[1:]:
                both(c, begins.index(d) - 1, finish)
        for c, d in active:
            if d in begins[1:k]:
                both(c, begins.index(d), begin)
        if len(first) < made:
            c = len(first)
            first[c] = tick
            both(c, 0, begin)
        left = WORK

        def can_make():
            if made == n:
                return False
            busy = sum(
                tall(c) == tall(made) and not (c in first and tick >= first[c] + begins[1]) for c in range(made)
            )
            return busy < (PARTS3 if tall(made) else PARTS) and all(x in done for x in make(made)[0])

        while left > 0:
            if can_make() and made - len(first) < 2:
                make(made)[1]()
                done.add(made)
                made += 1
                left -= 2.0
            elif items and all(x in done for x in items[0][1]):
                name, _, cost, act = items.pop(0)
                act()
                done.add(name)
                left -= cost
            else:
                break
            for name, after, act in list(waiting):
                if all(x in done for x in after):
                    waiting.remove((name, after, act))
                    act()
                    done.add(name)
        tick += 1
    need(*list(loads))


def backward(cube, tokens, weights, acts, cotangent):
    width, hidden = tokens.shape[1], weights[5].shape[1]
    chunks = backward_chunks(width, hidden)
    n, k = len(chunks), cube.k
    devices = 1 << k
    few, many = width // devices, hidden // devices
    landed = []
    for slots, count, cols in (((5, 9, 10), few, 512), ((width // 256,), many, 256)):
        for s in range(k):
            shape = (slots[min(s, len(slots) - 1)],) + (2,) * (k - 1 - s) + (count, cols)
            landed.append(pltpu.VMEM(shape, BF16))
    shapes = [(few, width)] * 5 + [(few, hidden)] * 2 + [(many, width)]
    outs = [jax.ShapeDtypeStruct(tokens.shape, BF16)] + [jax.ShapeDtypeStruct(s, F32) for s in shapes]
    square, broad = pltpu.VMEM(tokens.shape, BF16), pltpu.VMEM((SEQ, hidden), BF16)
    local_copies = len(KEPT) + 1 + hidden // 256 + 9 * (width // 256)
    acts = {**acts, **{name: acts[name].reshape(WIDE, -1, width) for name in ("q", "k")}}
    return pl.pallas_call(
        functools.partial(backward_kernel, cube, chunks),
        out_shape=tuple(outs),
        in_specs=[pl.BlockSpec(memory_space=pl.ANY)] * (10 + len(KEPT)),
        out_specs=tuple(
            [pl.BlockSpec(memory_space=pl.ANY)] + [pl.BlockSpec(memory_space=pltpu.VMEM)] * 8
        ),
        scratch_shapes=[broad] * 3
        + [square] * 5
        + [pltpu.VMEM(tokens.shape, F32)]
        + [
            pltpu.VMEM((TILES, 256, width), BF16),
            pltpu.VMEM((WIDE, 256, hidden), BF16),
            pltpu.VMEM((4, SEQ, 256), BF16),
            pltpu.VMEM((2, 128, 128), F32),
            pltpu.VMEM((2, SEQ // SPAN, 128, 128), BF16),
            pltpu.VMEM((PARTS,) + (2,) * k + (few, 512), BF16),
            pltpu.VMEM((PARTS3,) + (2,) * k + (many, 256), BF16),
            pltpu.SemaphoreType.DMA((n, k)),
            pltpu.SemaphoreType.DMA((n, k)),
            pltpu.SemaphoreType.DMA((local_copies,)),
        ]
        + landed,
        compiler_params=pltpu.CompilerParams(
            collective_id=1, has_side_effects=True, vmem_limit_bytes=64 * 1024 * 1024 - 65536
        ),
        name="backward_and_sum",
    )(cotangent, tokens, *weights, *(acts[name] for name in KEPT))


def hand_over_kernel(count, *refs):
    held, sems = refs[2 * count : 3 * count], refs[3 * count]
    come = [pltpu.make_async_copy(refs[i], held[i], sems.at[0, i]) for i in range(count)]
    go = [pltpu.make_async_copy(held[i], refs[count + i], sems.at[1, i]) for i in range(count)]
    for copy in come:
        copy.start()
    for i in range(count):
        come[i].wait()
        go[i].start()
    for copy in go:
        copy.wait()


def hand_over(*arrays):
    count = len(arrays)
    return pl.pallas_call(
        functools.partial(hand_over_kernel, count),
        out_shape=tuple(jax.ShapeDtypeStruct(a.shape, a.dtype) for a in arrays),
        in_specs=[pl.BlockSpec(memory_space=pl.ANY)] * count,
        out_specs=tuple([pl.BlockSpec(memory_space=pl.ANY)] * count),
        scratch_shapes=[pltpu.VMEM(a.shape, a.dtype) for a in arrays]
        + [pltpu.SemaphoreType.DMA((2, count))],
        compiler_params=pltpu.CompilerParams(vmem_limit_bytes=64 * 1024 * 1024 - 65536),
        name="hand_over",
    )(*arrays)


def local(cube, tokens, w_query, w_key, w_value, w_gate, w_out, w_one, w_two, w_three, cotangent):
    shards = (w_query, w_key, w_value, w_gate, w_out, w_one, w_two, w_three)
    gathered, acts = forward(cube, tokens, shards)
    weights = [w.reshape(-1, w.shape[-1]) for w in gathered]
    return hand_over(acts["out"], *backward(cube, tokens, weights, acts, cotangent))


def solution(mesh):
    nd, nf = mesh.shape["dp"], mesh.shape["fsdp"]
    rows = P(("dp", "fsdp"), None)

    def step(*args):
        fits = args[1].shape[0] % 16 == 0 and args[8].shape[0] % 8 == 0 and args[0].shape[0] == SEQ
        if fits:
            return local(Cube(nd, nf), *args)
        return plain_local(*args)

    return jax.shard_map(
        step, mesh=mesh, in_specs=(rows,) * 10, out_specs=(rows,) * 10, check_vma=False
    )
```
